256 devices in a mesh: dp: 8 (over x, core), cent: 32 (over y, z).
Axes of the slice: x: 4, y: 4, z: 8, core: 2. Of those that a mesh axis runs over, the one named last changes fastest.
Arguments:
- embeddings: bfloat16 [8192, 1536], P('dp'), may hold values from -1 to 1, as said below
- sharpness: float32 [8192], P('dp'), may hold values from 10 to 300
- centroids: bfloat16 [32768, 1536], P('cent'), may hold values from -1 to 1, as said below
Outputs:
- new_centroids: float32 [32768, 1536], P('cent', 'dp')
- residuals: bfloat16 [8192, 1536], P(('dp', 'cent'))
The draws below stay inside these ranges and needn't reach their ends.
Inputs may be any that keep to these rules, and one draw needn't show every extreme that they name: `embeddings`: each row has unit norm up to rounding. `centroids`: each row has unit norm up to rounding.
All inputs are finite; a program needn't handle non-finite values.
Results may differ from the reference program's by a relative error of at most 0.0034.
Values may be sent and summed in bfloat16 or wider, within the bound.
No kernel may reach another device: no remote copies, remote signals or barrier semaphores. Data moves between devices by JAX's collectives and lax.ppermute only.
A program may use at most 64 MiB of HBM per device.

```python
import jax
import jax.numpy as jnp
from jax import lax

D = 1536
CENTROIDS = 32768
ROWS = 8192
N_DP = 8


def unit_rows(values):
    return values / jnp.sqrt(jnp.sum(values * values, axis=1, keepdims=True))


def cluster_count():
    return max(CENTROIDS // 256, 16)


def cluster_frame(key):
    groups = cluster_count()
    centers = unit_rows(jax.random.normal(jax.random.fold_in(key, 21), (groups, D), jnp.float32))
    drifts = unit_rows(jax.random.normal(jax.random.fold_in(key, 22), (groups, D), jnp.float32))
    return (centers, drifts)


def centroid_table(key):
    centers, drifts = cluster_frame(key)
    member = jax.random.randint(jax.random.fold_in(key, 23), (CENTROIDS,), 0, cluster_count())
    level = jax.random.uniform(jax.random.fold_in(key, 24), (CENTROIDS,), jnp.float32)
    spread = jnp.exp(jnp.log(0.25) + level * (jnp.log(1.2) - jnp.log(0.25)))
    noise = jax.random.normal(jax.random.fold_in(key, 11), (CENTROIDS, D), jnp.float32) * D ** (-0.5)
    return unit_rows(centers[member] + spread[:, None] * noise)


def draw_centroids(key, part):
    return centroid_table(key).astype(jnp.bfloat16)


def draw_embeddings(key, part):
    centers, drifts = cluster_frame(key)
    member = jax.random.randint(jax.random.fold_in(key, 25), (ROWS,), 0, cluster_count())
    noise = jax.random.normal(jax.random.fold_in(key, 12), (ROWS, D), jnp.float32) * D ** (-0.5)
    values = unit_rows(centers[member] + 0.5 * drifts[member] + 0.6 * noise)
    return values.astype(jnp.bfloat16)


def draw_sharpness(key, part):
    base = jax.random.uniform(jax.random.fold_in(key, 15), (ROWS,), jnp.float32)
    values = jnp.exp(jnp.log(10.0) + base * (jnp.log(100.0) - jnp.log(10.0)))
    return values


def setup_inputs(seed: int = 0) -> dict:
    splits = jax.random.split(jax.random.key(seed), 4)
    return {
        "embeddings": draw_embeddings(jax.random.fold_in(splits[3], 71), 0),
        "sharpness": draw_sharpness(jax.random.fold_in(splits[3], 71), 0),
        "centroids": draw_centroids(jax.random.fold_in(splits[3], 71), 0),
    }


def reference(embeddings, sharpness, centroids):
    rows_block = ROWS // N_DP
    emb_blocks = embeddings.reshape(N_DP, rows_block, D)
    sharp_blocks = sharpness.reshape(N_DP, rows_block)

    def step(carry, item):
        counts, update = carry
        block, sharp = item
        scores = jnp.dot(block, centroids.T, preferred_element_type=jnp.float32) * sharp[:, None]
        row_top = lax.optimization_barrier(jnp.max(scores, axis=1))
        weights = jnp.exp(scores - row_top[:, None])
        row_total = lax.optimization_barrier(jnp.sum(weights, axis=1))
        responsibility = (weights / row_total[:, None]).astype(jnp.bfloat16)
        mixture = jnp.dot(responsibility, centroids, preferred_element_type=jnp.float32)
        residual = (block.astype(jnp.float32) - mixture).astype(jnp.bfloat16)
        counts = counts + lax.optimization_barrier(jnp.sum(responsibility.astype(jnp.float32), axis=0))
        update = update + jnp.dot(responsibility.T, residual, preferred_element_type=jnp.float32)
        return ((counts, update), residual)
    init = (jnp.zeros((CENTROIDS,), jnp.float32), jnp.zeros((CENTROIDS, D), jnp.float32))
    (counts, update), residuals = lax.scan(step, init, (emb_blocks, sharp_blocks))
    moved = centroids.astype(jnp.float32) + update / (counts[:, None] + 1.0)
    new_centroids = moved * lax.rsqrt(lax.optimization_barrier(jnp.sum(moved * moved, axis=1)) + 1e-06)[:, None]
    return (new_centroids, residuals.reshape(ROWS, D))
```

```python
import functools

import jax
import jax.numpy as jnp
from jax import lax
from jax.experimental import pallas as pl
from jax.experimental.pallas import tpu as pltpu
from jax.sharding import Mesh
from jax.sharding import PartitionSpec as P

BF16, F32 = jnp.bfloat16, jnp.float32
VMEM = pl.BlockSpec(memory_space=pltpu.VMEM)
PARAMS = pltpu.CompilerParams(vmem_limit_bytes=56 << 20)


def call(kernel, outs, *args, scratch=()):
    return pl.pallas_call(
        kernel,
        out_shape=[jax.ShapeDtypeStruct(s, d) for s, d in outs],
        in_specs=[VMEM] * len(args),
        out_specs=[VMEM] * len(outs),
        scratch_shapes=[pltpu.VMEM(s, d) for s, d in scratch],
        compiler_params=PARAMS,
    )(*args)


def to_column(row):
    return jnp.broadcast_to(row, (128, row.shape[1])).T[:, :1]


def to_row(column):
    return jnp.broadcast_to(column, (column.shape[0], 128)).T[:1, :]


def swap_cores(a):
    return lax.ppermute(a, "c", [(0, 1), (1, 0)])


def cube(a, axis, masks):
    pairs = [(c, i, i ^ masks[c]) for c in range(2) for i in range(4)]
    if axis == "x":
        return lax.ppermute(a, ("x", "c"), [(i * 2 + c, j * 2 + c) for c, i, j in pairs])
    return lax.ppermute(a, ("c", axis), [(c * 4 + i, c * 4 + j) for c, i, j in pairs])


FIRST, SECOND = (1, 3), (3, 1)


def shifted(a, by):
    return lax.ppermute(
        a, ("c", "z"), [(c * 8 + i, c * 8 + (i + by[c]) % 8) for c in range(2) for i in range(8)]
    )


SLOTS = ((1, 2, 3, 4), (-1, -2, -3, 0))


def slot_shift(slot):
    return tuple(SLOTS[c][slot] for c in range(2))


def scores_kernel(e_ref, c_ref, sharp_ref, s_ref, lse_ref):
    sharp = to_column(sharp_ref[...])
    s = lax.dot_general(
        e_ref[...], c_ref[...], (((1,), (1,)), ((), ())), preferred_element_type=F32
    )
    s = s * sharp
    s_ref[...] = s
    top = jnp.max(s, axis=1, keepdims=True)
    total = jnp.sum(jnp.exp(s - top), axis=1, keepdims=True)
    lse_ref[...] = to_row(top + jnp.log(total))


def scores(e, c, sharp):
    rows, d = e.shape
    k = c.shape[0]
    b = 256
    return pl.pallas_call(
        scores_kernel,
        grid=(rows // b,),
        out_shape=[jax.ShapeDtypeStruct((rows, k), F32), jax.ShapeDtypeStruct((1, rows), F32)],
        in_specs=[
            pl.BlockSpec((b, d), lambda i: (i, 0)),
            pl.BlockSpec((k, d), lambda i: (0, 0)),
            pl.BlockSpec((1, b), lambda i: (0, i)),
        ],
        out_specs=[pl.BlockSpec((b, k), lambda i: (i, 0)), pl.BlockSpec((1, b), lambda i: (0, i))],
        compiler_params=PARAMS,
    )(e, c, sharp.reshape(1, rows))


def natural_block(core, place, slot):
    y, z = lax.axis_index("y"), lax.axis_index("z")
    first = jnp.where(core == 0, 1, 3)
    second = jnp.where(core == 0, 3, 1)
    mask = (0, second, first, 2)[place]
    shift = jnp.where(core == 0, SLOTS[0][slot], SLOTS[1][slot])
    return lax.bitwise_xor(y, mask) * 8 + lax.rem(z + shift + 8, 8)


def resp_kernel(s_ref, lse_ref, keep_ref, send_ref, col_ref):
    for r in range(4):
        row = lse_ref[:, r * 256 : r * 256 + 256]
        col_ref[r * 256 : r * 256 + 256, :] = jnp.broadcast_to(row, (128, 256)).T
    core = lax.axis_index("c")
    for out, owner in ((send_ref, 1 - core), (keep_ref, core)):
        for place in range(4):
            for slot in range(4):
                at = pl.multiple_of(natural_block(owner, place, slot) * 32, 32)
                s = s_ref[pl.ds(at, 32), :]
                lse = col_ref[pl.ds(at, 32), :][:, :1]
                out[place, slot] = jnp.exp(s - lse).astype(BF16)


def mixture_kernel(places, own_ref, oth_ref, c_ref, *outs):
    for half, ref in enumerate((own_ref, oth_ref)):
        for out, place in zip(outs, places):
            part = jnp.dot(
                ref[place].reshape(128, -1), c_ref[...], preferred_element_type=F32
            )
            out[:, half] = part.reshape(4, 32, -1).astype(out.dtype)


def turn_kernel(own_ref, oth_ref, rt_ref, cnt_ref):
    total = jnp.zeros((1, 1024), F32)
    for place in range(4):
        for half, ref in enumerate((own_ref, oth_ref)):
            at = place * 256 + half * 128
            r = ref[place].reshape(128, 1024)
            rt_ref[:, at : at + 128] = r.T
            total = total + jnp.sum(r.astype(F32), axis=0, keepdims=True)
    cnt_ref[...] = total


def gathered(refs, g_ref):
    for n, ref in enumerate(refs):
        for half in range(2):
            at = n * 256 + half * 128
            g_ref[at : at + 128, :] = ref[:, half].reshape(128, -1)


def update_first_kernel(rt_ref, g0_ref, g1_ref, u_ref, g_ref):
    gathered((g0_ref, g1_ref), g_ref)
    for r in range(4):
        at = r * 256
        u_ref[at : at + 256, :] = jnp.dot(
            rt_ref[at : at + 256, :512], g_ref[...], preferred_element_type=F32
        )


def update_last_kernel(rt_ref, g2_ref, g3_ref, u_ref, cnt_ref, c_ref, keep_ref, send_ref, g_ref, cnt_s):
    gathered((g2_ref, g3_ref), g_ref)
    for r in range(4):
        row = cnt_ref[:, r * 256 : r * 256 + 256]
        cnt_s[r * 256 : r * 256 + 256, :] = jnp.broadcast_to(row, (128, 256)).T
    core = lax.axis_index("c")
    for out, half in ((send_ref, 1 - core), (keep_ref, core)):
        for r in range(2):
            at = pl.multiple_of(half * 512 + r * 256, 256)
            rows = pl.ds(at, 256)
            u = u_ref[rows, :] + jnp.dot(
                rt_ref[rows, 512:], g_ref[...], preferred_element_type=F32
            )
            u = u + cnt_s[rows, :][:, :1] * c_ref[rows, :].astype(F32)
            out[r * 256 : r * 256 + 256, :] = u.astype(out.dtype)


def split_kernel(keep_ref, recv_ref, p0_ref, p1_ref, p2_ref, p3_ref):
    core, x = lax.axis_index("c"), lax.axis_index("x")
    first = jnp.where(core == 0, 1, 3)
    second = jnp.where(core == 0, 3, 1)
    for out, mask in ((p3_ref, 2), (p2_ref, first), (p1_ref, second), (p0_ref, 0)):
        cols = pl.ds(pl.multiple_of(lax.bitwise_xor(x, mask) * 384, 128), 384)
        out[...] = (keep_ref[:, cols] + recv_ref[:, cols].astype(F32)).astype(out.dtype)


def moved_kernel(c_ref, p0_ref, a_ref, b_ref, cnt_ref, moved_ref, stat_ref):
    core, x = lax.axis_index("c"), lax.axis_index("x")
    rows = pl.ds(pl.multiple_of(core * 512, 512), 512)
    cols = pl.ds(pl.multiple_of(x * 384, 128), 384)
    moved = c_ref[rows, cols].astype(F32) + p0_ref[...]
    moved = moved + a_ref[...].astype(F32) + b_ref[...].astype(F32)
    moved_ref[...] = moved
    square = to_row(jnp.sum(moved * moved, axis=1, keepdims=True))
    count = jnp.where(core == 0, cnt_ref[:, :512], cnt_ref[:, 512:])
    stat_ref[...] = jnp.concatenate([square, count], axis=0)


def final_kernel(moved_ref, s0_ref, s1_ref, s2_ref, s3_ref, keep_ref, send_ref):
    stat = s0_ref[...] + s1_ref[...] + s2_ref[...] + s3_ref[...]
    grown = 1.0 + stat[1:2]
    scale = to_column(lax.rsqrt(stat[:1] + 1e-06 * grown * grown))
    new = moved_ref[...] * scale
    low, high = new[:, :192], new[:, 192:]
    core = lax.axis_index("c")
    keep_ref[...] = jnp.where(core == 0, low, high)
    send_ref[...] = jnp.where(core == 0, high, low)


def merged_lse(lse):
    copies = jnp.broadcast_to(lse, (32, *lse.shape))
    every = lax.all_to_all(copies, ("y", "z"), split_axis=0, concat_axis=0, tiled=True)
    top = jnp.max(every, axis=0)
    return top + jnp.log(jnp.sum(jnp.exp(every - top), axis=0))


def per_device(embeddings, sharpness, centroids):
    d = embeddings.shape[1]
    s, lse = scores(embeddings, centroids, sharpness)
    lse = merged_lse(lse)
    block = (4, 4, 32, 1024)
    keep, send = call(
        resp_kernel, [(block, BF16)] * 2, s, lse, scratch=[((1024, 128), F32)]
    )
    other = swap_cores(send)
    part = (4, 2, 32, d)
    m3, m2 = call(
        functools.partial(mixture_kernel, (3, 2)), [(part, BF16)] * 2, keep, other, centroids
    )
    r3 = cube(m3, "y", FIRST)
    r2 = cube(m2, "y", FIRST)
    m1, m0 = call(
        functools.partial(mixture_kernel, (1, 0)), [(part, F32)] * 2, keep, other, centroids
    )
    r1 = cube((m1 + r3.astype(F32)).astype(BF16), "y", SECOND)
    rt, cnt = call(turn_kernel, [((1024, 1024), BF16), ((1, 1024), F32)], keep, other)
    cnt = cnt + swap_cores(cnt)
    summed = (m0 + r2.astype(F32) + r1.astype(F32)).astype(BF16)
    got = [shifted(summed[t], slot_shift(t)) for t in range(4)]
    both = sum(g.astype(F32) for g in got)
    mixture = both[0] + swap_cores(both[1])
    start = (lax.axis_index("y") * 8 + lax.axis_index("z")) * 32
    own_rows = lax.dynamic_slice_in_dim(embeddings, start, 32, 0)
    residual = (own_rows.astype(F32) - mixture).astype(BF16)
    pair = jnp.stack([residual, swap_cores(residual)])
    g0 = jnp.stack([shifted(pair, tuple(-b for b in slot_shift(t))) for t in range(4)])
    g1 = cube(g0, "y", SECOND)
    g2 = cube(g0, "y", FIRST)
    g3 = cube(g1, "y", FIRST)
    (u,) = call(
        update_first_kernel, [((1024, d), F32)], rt, g0, g1, scratch=[((512, d), BF16)]
    )
    keep_u, send_u = call(
        update_last_kernel,
        [((512, d), F32), ((512, d), BF16)],
        rt, g2, g3, u, cnt * 0.5, centroids,
        scratch=[((512, d), BF16), ((1024, 128), F32)],
    )
    p0, p1, p2, p3 = call(
        split_kernel,
        [((512, 384), F32), ((512, 384), F32), ((512, 384), BF16), ((512, 384), BF16)],
        keep_u, swap_cores(send_u),
    )
    q3 = cube(p3, "x", FIRST)
    q2 = cube(p2, "x", FIRST)
    q1 = cube((p1 + q3.astype(F32)).astype(BF16), "x", SECOND)
    moved, stat = call(
        moved_kernel, [((512, 384), F32), ((2, 512), F32)], centroids, p0, q2, q1, cnt
    )
    others = [
        lax.ppermute(stat, "x", [(i, (i + n) % 4) for i in range(4)]) for n in (1, 2, 3)
    ]
    kept, sent = call(final_kernel, [((512, 192), F32)] * 2, moved, stat, *others)
    came = swap_cores(sent)
    low = lax.axis_index("c") == 0
    new = jnp.concatenate([jnp.where(low, kept, came), jnp.where(low, came, kept)])
    return (new, residual)


def solution(mesh):
    split = Mesh(mesh.devices.reshape(4, 2, 4, 8), ("x", "c", "y", "z"))
    rows, cents = ("x", "c"), ("y", "z")
    return jax.shard_map(
        per_device,
        mesh=split,
        in_specs=(P(rows, None), P(rows), P(cents, None)),
        out_specs=(P(cents, rows), P(rows + cents, None)),
        check_vma=False,
    )
```

```python
import functools

import jax
import jax.numpy as jnp
from jax import lax
from jax.experimental import pallas as pl
from jax.experimental.pallas import tpu as pltpu
from jax.sharding import Mesh
from jax.sharding import PartitionSpec as P

BF16, F32 = jnp.bfloat16, jnp.float32
VMEM = pl.BlockSpec(memory_space=pltpu.VMEM)
PARAMS = pltpu.CompilerParams(vmem_limit_bytes=20 << 20)


def near(a):
    return pltpu.with_memory_space_constraint(a, pltpu.VMEM)


def call(kernel, outs, *args, scratch=()):
    return pl.pallas_call(
        kernel,
        out_shape=[pltpu.VMEM(s, d) for s, d in outs],
        in_specs=[VMEM] * len(args),
        out_specs=[VMEM] * len(outs),
        scratch_shapes=[pltpu.VMEM(s, d) for s, d in scratch],
        compiler_params=PARAMS,
    )(*(near(a) for a in args))


def to_column(row):
    return jnp.broadcast_to(row, (128, row.shape[1])).T[:, :1]


def to_row(column):
    return jnp.broadcast_to(column, (column.shape[0], 128)).T[:1, :]


def swap_cores(a):
    return lax.ppermute(a, "c", [(0, 1), (1, 0)])


def cube(a, axis, masks):
    pairs = [(c, i, i ^ masks[c]) for c in range(2) for i in range(4)]
    if axis == "x":
        return lax.ppermute(a, ("x", "c"), [(i * 2 + c, j * 2 + c) for c, i, j in pairs])
    return lax.ppermute(a, ("c", axis), [(c * 4 + i, c * 4 + j) for c, i, j in pairs])


FIRST, SECOND = (1, 3), (3, 1)


def shifted(a, by):
    return lax.ppermute(
        a, ("c", "z"), [(c * 8 + i, c * 8 + (i + by[c]) % 8) for c in range(2) for i in range(8)]
    )


SLOTS = ((1, 2, 3, 4), (-1, -2, -3, 0))


def slot_shift(slot):
    return tuple(SLOTS[c][slot] for c in range(2))


def scores_kernel(e_hbm, c_hbm, sharp_ref, s_ref, lse_ref, c_ref, e_ref, sems):
    def fetch(n):
        ref, hbm, at = (e_ref, e_hbm, n) if n < 4 else (c_ref, c_hbm, n - 4)
        rows = pl.ds(at * 256, 256)
        return pltpu.make_async_copy(hbm.at[rows], ref.at[rows], sems.at[n])

    for n in (0, 4, 5, 6, 7, 1, 2, 3):
        fetch(n).start()
    for r in range(4):
        fetch(r).wait()
        rows = slice(r * 256, r * 256 + 256)
        sharp = to_column(sharp_ref[:, rows])
        for k in range(4):
            if r == 0:
                fetch(4 + k).wait()
            cols = slice(k * 256, k * 256 + 256)
            part = lax.dot_general(
                e_ref[rows, :], c_ref[cols, :], (((1,), (1,)), ((), ())),
                preferred_element_type=F32,
            )
            s_ref[rows, cols] = part * sharp
        s = s_ref[rows, :]
        top = jnp.max(s, axis=1, keepdims=True)
        total = jnp.sum(jnp.exp(s - top), axis=1, keepdims=True)
        lse_ref[:, rows] = to_row(top + jnp.log(total))


def scores(e, c, sharp):
    rows, d = e.shape
    k = c.shape[0]
    far = pl.BlockSpec(memory_space=pltpu.HBM)
    outs = [((rows, k), F32), ((1, rows), F32), ((k, d), BF16)]
    return pl.pallas_call(
        scores_kernel,
        out_shape=[pltpu.VMEM(s, t) for s, t in outs],
        in_specs=[far, far, VMEM],
        out_specs=[VMEM] * 3,
        scratch_shapes=[pltpu.VMEM((rows, d), BF16), pltpu.SemaphoreType.DMA((8,))],
        compiler_params=PARAMS,
    )(e, c, sharp.reshape(1, rows))


def natural_block(core, place, slot):
    y, z = lax.axis_index("y"), lax.axis_index("z")
    first = jnp.where(core == 0, 1, 3)
    second = jnp.where(core == 0, 3, 1)
    mask = (0, second, first, 2)[place]
    shift = jnp.where(core == 0, SLOTS[0][slot], SLOTS[1][slot])
    return lax.bitwise_xor(y, mask) * 8 + lax.rem(z + shift + 8, 8)


def columns_of(row_ref, col_ref):
    for r in range(0, row_ref.shape[1], 256):
        row = row_ref[:, r : r + 256]
        col_ref[r : r + 256, :] = jnp.broadcast_to(row, (128, 256)).T


def rows_at(core, place, slot):
    return pl.ds(pl.multiple_of(natural_block(core, place, slot) * 32, 32), 32)


def weights_kernel(s_ref, lse_ref, keep_ref, send_ref, col_ref):
    columns_of(lse_ref, col_ref)
    core = lax.axis_index("c")
    for out, owner in ((send_ref, 1 - core), (keep_ref, core)):
        for place in range(4):
            for slot in range(4):
                rows = rows_at(owner, place, slot)
                out[place, slot] = jnp.exp(s_ref[rows, :] - col_ref[rows, :][:, :1]).astype(BF16)


def mixture_kernel(place, own_ref, oth_ref, c_ref, *outs):
    for n, out in enumerate(outs):
        for half, ref in enumerate((own_ref, oth_ref)):
            part = jnp.dot(
                ref[place + n].reshape(128, -1), c_ref[...], preferred_element_type=F32
            )
            out[:, half] = part.reshape(4, 32, -1)


def share_kernel(places, own_row, oth_row, *refs):
    cols = refs[-2:]
    ins, outs = refs[: len(places)], refs[len(places) : 2 * len(places)]
    core = lax.axis_index("c")
    for row, col in zip((own_row, oth_row), cols):
        columns_of(row, col)
    for place, raw, out in zip(places, ins, outs):
        for slot in range(4):
            rows = rows_at(core, place, slot)
            for half, col in enumerate(cols):
                out[slot, half] = (raw[slot, half] * col[rows, :][:, :1]).astype(out.dtype)


def turn_kernel(own_ref, oth_ref, own_row, oth_row, rt_ref, cnt_ref, own_col, oth_col):
    total = jnp.zeros((1, 1024), F32)
    core = lax.axis_index("c")
    columns_of(own_row, own_col)
    columns_of(oth_row, oth_col)
    for place in range(4):
        for half, (ref, col) in enumerate(((own_ref, own_col), (oth_ref, oth_col))):
            at = place * 256 + half * 128
            parts = [
                ref[place, slot].astype(F32) * col[rows_at(core, place, slot), :][:, :1]
                for slot in range(4)
            ]
            r = jnp.concatenate(parts).astype(BF16)
            rt_ref[:, at : at + 128] = r.T
            total = total + jnp.sum(r.astype(F32), axis=0, keepdims=True)
    cnt_ref[...] = total


def gathered(refs, g_ref):
    for n, ref in enumerate(refs):
        for half in range(2):
            at = n * 256 + half * 128
            g_ref[at : at + 128, :] = ref[:, half].reshape(128, -1)


def update_first_kernel(rt_ref, g0_ref, g1_ref, u_ref, g_ref):
    gathered((g0_ref, g1_ref), g_ref)
    for r in range(4):
        at = r * 256
        u_ref[at : at + 256, :] = jnp.dot(
            rt_ref[at : at + 256, :512], g_ref[...], preferred_element_type=F32
        )


def update_last_kernel(rt_ref, g2_ref, g3_ref, u_ref, cnt_ref, c_ref, keep_ref, send_ref, g_ref, cnt_s):
    gathered((g2_ref, g3_ref), g_ref)
    columns_of(cnt_ref, cnt_s)
    core = lax.axis_index("c")
    for out, half in ((send_ref, 1 - core), (keep_ref, core)):
        for r in range(2):
            at = pl.multiple_of(half * 512 + r * 256, 256)
            rows = pl.ds(at, 256)
            u = u_ref[rows, :] + jnp.dot(
                rt_ref[rows, 512:], g_ref[...], preferred_element_type=F32
            )
            u = u + cnt_s[rows, :][:, :1] * c_ref[rows, :].astype(F32)
            out[r * 256 : r * 256 + 256, :] = u.astype(out.dtype)


def split_kernel(keep_ref, recv_ref, p0_ref, p1_ref, p2_ref, p3_ref):
    core, x = lax.axis_index("c"), lax.axis_index("x")
    first = jnp.where(core == 0, 1, 3)
    second = jnp.where(core == 0, 3, 1)
    for out, mask in ((p3_ref, 2), (p2_ref, first), (p1_ref, second), (p0_ref, 0)):
        cols = pl.ds(pl.multiple_of(lax.bitwise_xor(x, mask) * 384, 128), 384)
        out[...] = (keep_ref[:, cols] + recv_ref[:, cols].astype(F32)).astype(out.dtype)


def moved_kernel(c_ref, p0_ref, a_ref, b_ref, cnt_ref, moved_ref, stat_ref):
    core, x = lax.axis_index("c"), lax.axis_index("x")
    rows = pl.ds(pl.multiple_of(core * 512, 512), 512)
    cols = pl.ds(pl.multiple_of(x * 384, 128), 384)
    moved = c_ref[rows, cols].astype(F32) + p0_ref[...]
    moved = moved + a_ref[...].astype(F32) + b_ref[...].astype(F32)
    moved_ref[...] = moved
    square = to_row(jnp.sum(moved * moved, axis=1, keepdims=True))
    count = jnp.where(core == 0, cnt_ref[:, :512], cnt_ref[:, 512:])
    stat_ref[...] = jnp.concatenate([square, count], axis=0)


def final_kernel(moved_ref, s0_ref, s1_ref, s2_ref, s3_ref, keep_ref, send_ref):
    stat = s0_ref[...] + s1_ref[...] + s2_ref[...] + s3_ref[...]
    grown = 1.0 + stat[1:2]
    scale = to_column(lax.rsqrt(stat[:1] + 1e-06 * grown * grown))
    new = moved_ref[...] * scale
    low, high = new[:, :192], new[:, 192:]
    core = lax.axis_index("c")
    keep_ref[...] = jnp.where(core == 0, low, high)
    send_ref[...] = jnp.where(core == 0, high, low)


def merged_lse(lse):
    copies = jnp.broadcast_to(lse, (32, *lse.shape))
    every = lax.all_to_all(copies, ("y", "z"), split_axis=0, concat_axis=0, tiled=True)
    top = jnp.max(every, axis=0)
    return top + jnp.log(jnp.sum(jnp.exp(every - top), axis=0))


def per_device(embeddings, sharpness, centroids):
    d = embeddings.shape[1]
    s, local, near_c = scores(embeddings, centroids, sharpness)
    block = (4, 4, 32, 1024)
    wide = ((1024, 128), F32)
    keep, send = call(weights_kernel, [(block, BF16)] * 2, s, local, scratch=[wide])
    share = jnp.exp(local - merged_lse(local))
    other = swap_cores(send)
    share_other = swap_cores(share)
    part = (4, 2, 32, d)
    raw2, raw3 = call(
        functools.partial(mixture_kernel, 2), [(part, F32)] * 2, keep, other, near_c
    )
    m3, m2 = call(
        functools.partial(share_kernel, (3, 2)), [(part, BF16)] * 2,
        share, share_other, raw3, raw2, scratch=[wide] * 2,
    )
    r3 = cube(m3, "y", FIRST)
    r2 = cube(m2, "y", FIRST)
    raw0, raw1 = call(
        functools.partial(mixture_kernel, 0), [(part, F32)] * 2, keep, other, near_c
    )
    m1, m0 = call(
        functools.partial(share_kernel, (1, 0)), [(part, F32)] * 2,
        share, share_other, raw1, raw0, scratch=[wide] * 2,
    )
    r1 = cube((m1 + r3.astype(F32)).astype(BF16), "y", SECOND)
    rt, cnt = call(
        turn_kernel, [((1024, 1024), BF16), ((1, 1024), F32)],
        keep, other, share, share_other, scratch=[wide] * 2,
    )
    m0, rt, cnt = lax.optimization_barrier((m0, rt, cnt))
    summed = (m0 + r2.astype(F32) + r1.astype(F32)).astype(BF16)
    got = [shifted(summed[t], slot_shift(t)) for t in range(4)]
    both = sum(g.astype(F32) for g in got)
    mixture = both[0] + swap_cores(both[1])
    start = (lax.axis_index("y") * 8 + lax.axis_index("z")) * 32
    own_rows = lax.dynamic_slice_in_dim(embeddings, start, 32, 0)
    residual = (own_rows.astype(F32) - mixture).astype(BF16)
    cnt = cnt + swap_cores(cnt)
    pair = jnp.stack([residual, swap_cores(residual)])
    g0 = jnp.stack([shifted(pair, tuple(-b for b in slot_shift(t))) for t in range(4)])
    g1 = cube(g0, "y", SECOND)
    g1, g0 = lax.optimization_barrier((g1, g0))
    g3 = cube(g1, "y", FIRST)
    g2 = cube(g0, "y", FIRST)
    (u,) = call(
        update_first_kernel, [((1024, d), F32)], rt, g0, g1, scratch=[((512, d), BF16)]
    )
    keep_u, send_u = call(
        update_last_kernel,
        [((512, d), F32), ((512, d), BF16)],
        rt, g2, g3, u, cnt * 0.5, near_c,
        scratch=[((512, d), BF16), ((1024, 128), F32)],
    )
    p0, p1, p2, p3 = call(
        split_kernel,
        [((512, 384), F32), ((512, 384), F32), ((512, 384), BF16), ((512, 384), BF16)],
        keep_u, swap_cores(send_u),
    )
    q3 = cube(p3, "x", FIRST)
    q2 = cube(p2, "x", FIRST)
    q1 = cube((p1 + q3.astype(F32)).astype(BF16), "x", SECOND)
    moved, stat = call(
        moved_kernel, [((512, 384), F32), ((2, 512), F32)], near_c, p0, q2, q1, cnt
    )
    others = [
        lax.ppermute(stat, "x", [(i, (i + n) % 4) for i in range(4)]) for n in (1, 2, 3)
    ]
    kept, sent = call(final_kernel, [((512, 192), F32)] * 2, moved, stat, *others)
    came = swap_cores(sent)
    low = lax.axis_index("c") == 0
    new = jnp.concatenate([jnp.where(low, kept, came), jnp.where(low, came, kept)])
    return (new, residual)


def solution(mesh):
    split = Mesh(mesh.devices.reshape(4, 2, 4, 8), ("x", "c", "y", "z"))
    rows, cents = ("x", "c"), ("y", "z")
    return jax.shard_map(
        per_device,
        mesh=split,
        in_specs=(P(rows, None), P(rows), P(cents, None)),
        out_specs=(P(cents, rows), P(rows + cents, None)),
        check_vma=False,
    )
```

```python
import functools

import jax
import jax.numpy as jnp
from jax import lax
from jax.experimental import pallas as pl
from jax.experimental.pallas import tpu as pltpu
from jax.sharding import Mesh
from jax.sharding import PartitionSpec as P

BF16, F32 = jnp.bfloat16, jnp.float32
VMEM = pl.BlockSpec(memory_space=pltpu.VMEM)
PARAMS = pltpu.CompilerParams(vmem_limit_bytes=20 << 20)


def near(a):
    return pltpu.with_memory_space_constraint(a, pltpu.VMEM)


def call(kernel, outs, *args, scratch=()):
    return pl.pallas_call(
        kernel,
        out_shape=[pltpu.VMEM(s, d) for s, d in outs],
        in_specs=[VMEM] * len(args),
        out_specs=[VMEM] * len(outs),
        scratch_shapes=[pltpu.VMEM(s, d) for s, d in scratch],
        compiler_params=PARAMS,
    )(*(near(a) for a in args))


def to_column(row):
    return jnp.broadcast_to(row, (128, row.shape[1])).T[:, :1]


def to_row(column):
    return jnp.broadcast_to(column, (column.shape[0], 128)).T[:1, :]


def swap_cores(a):
    return lax.ppermute(a, "c", [(0, 1), (1, 0)])


def cube(a, axis, masks):
    pairs = [(c, i, i ^ masks[c]) for c in range(2) for i in range(4)]
    if axis == "x":
        return lax.ppermute(a, ("x", "c"), [(i * 2 + c, j * 2 + c) for c, i, j in pairs])
    return lax.ppermute(a, ("c", axis), [(c * 4 + i, c * 4 + j) for c, i, j in pairs])


FIRST, SECOND = (1, 3), (3, 1)


def shifted(a, by):
    return lax.ppermute(
        a, ("c", "z"), [(c * 8 + i, c * 8 + (i + by[c]) % 8) for c in range(2) for i in range(8)]
    )


SLOTS = ((1, 2, 3, 4), (-1, -2, -3, 0))


def slot_shift(slot):
    return tuple(SLOTS[c][slot] for c in range(2))


EXT = 128
STREAMS = ((0, 384),)
WIDTHS = tuple(4 * w for _, w in STREAMS)


def lse_of(ref, *at):
    ext = ref[(*at, slice(None), slice(-EXT, None))] if at else ref[...][..., -EXT:]
    ext = ext.reshape(-1, EXT).astype(F32)
    return jnp.sum(ext, axis=1, keepdims=True)


def pieces(value, count):
    lane = lax.broadcasted_iota(jnp.int32, (value.shape[0], EXT), 1)
    out = jnp.zeros(lane.shape, F32)
    for n in range(count):
        part = value.astype(BF16).astype(F32)
        out = jnp.where(lane == n, part, out)
        value = value - part
    return out.astype(BF16)


def merged(values, logs):
    top = functools.reduce(jnp.maximum, logs)
    parts = [jnp.exp(one - top) for one in logs]
    total = sum(parts)
    inverse = 1.0 / total
    value = sum(v * (p * inverse) for v, p in zip(values, parts))
    return value, top + jnp.log(total)


def scores_kernel(e_hbm, c_hbm, sharp_ref, s_ref, lse_ref, own_ref, *rest):
    cols_refs, (e_ref, c_ref, sems, col_sems) = rest[:-4], rest[-4:]

    def fetch(n):
        ref, hbm, at = (e_ref, e_hbm, n) if n < 4 else (c_ref, c_hbm, n - 4)
        rows = pl.ds(at * 256, 256)
        return pltpu.make_async_copy(hbm.at[rows], ref.at[rows], sems.at[n])

    for n in (0, 4, 5, 6, 7, 1, 2, 3):
        fetch(n).start()
    copies = []
    for n, (ref, (off, width)) in enumerate(zip(cols_refs, STREAMS)):
        for x in range(4):
            copies.append(
                pltpu.make_async_copy(
                    c_hbm.at[:, pl.ds(384 * x + off, width)],
                    ref.at[:, pl.ds(width * x, width)],
                    col_sems.at[n * 4 + x],
                )
            )
    for copy in copies:
        copy.start()
    for r in range(4):
        fetch(r).wait()
        rows = slice(r * 256, r * 256 + 256)
        sharp = to_column(sharp_ref[:, rows])
        for k in range(4):
            if r == 0:
                fetch(4 + k).wait()
            cols = slice(k * 256, k * 256 + 256)
            part = lax.dot_general(
                e_ref[rows, :], c_ref[cols, :], (((1,), (1,)), ((), ())),
                preferred_element_type=F32,
            )
            s_ref[rows, cols] = part * sharp
        s = s_ref[rows, :]
        top = jnp.max(s, axis=1, keepdims=True)
        total = jnp.sum(jnp.exp(s - top), axis=1, keepdims=True)
        lse_ref[:, rows] = to_row(top + jnp.log(total))
    at = (lax.axis_index("y") * 8 + lax.axis_index("z")) * 32
    own_ref[...] = e_ref[pl.ds(pl.multiple_of(at, 32), 32), :]
    for copy in copies:
        copy.wait()


def scores(e, c, sharp):
    rows, d = e.shape
    k = c.shape[0]
    far = pl.BlockSpec(memory_space=pltpu.HBM)
    outs = [((rows, k), F32), ((1, rows), F32), ((32, d), BF16)]
    outs += [((k, w), BF16) for w in WIDTHS]
    hbm = [pltpu.with_memory_space_constraint(a, pltpu.HBM) for a in (e, c)]
    return pl.pallas_call(
        scores_kernel,
        out_shape=[pltpu.VMEM(s, t) for s, t in outs],
        in_specs=[far, far, VMEM],
        out_specs=[VMEM] * len(outs),
        scratch_shapes=[
            pltpu.VMEM((rows, d), BF16),
            pltpu.VMEM((k, d), BF16),
            pltpu.SemaphoreType.DMA((8,)),
            pltpu.SemaphoreType.DMA((4 * len(STREAMS),)),
        ],
        compiler_params=PARAMS,
    )(*hbm, sharp.reshape(1, rows))


def natural_block(core, place, slot):
    y, z = lax.axis_index("y"), lax.axis_index("z")
    first = jnp.where(core == 0, 1, 3)
    second = jnp.where(core == 0, 3, 1)
    mask = (0, second, first, 2)[place]
    shift = jnp.where(core == 0, SLOTS[0][slot], SLOTS[1][slot])
    return lax.bitwise_xor(y, mask) * 8 + lax.rem(z + shift + 8, 8)


def columns_of(row_ref, col_ref):
    for r in range(0, row_ref.shape[1], 256):
        row = row_ref[:, r : r + 256]
        col_ref[r : r + 256, :] = jnp.broadcast_to(row, (128, 256)).T


def rows_at(core, place, slot):
    return pl.ds(pl.multiple_of(natural_block(core, place, slot) * 32, 32), 32)


def weights_kernel(s_ref, lse_ref, keep_ref, send_ref, col_ref):
    columns_of(lse_ref, col_ref)
    core = lax.axis_index("c")
    for out, owner in ((send_ref, 1 - core), (keep_ref, core)):
        for place in range(4):
            for slot in range(4):
                rows = rows_at(owner, place, slot)
                out[place, slot] = jnp.exp(s_ref[rows, :] - col_ref[rows, :][:, :1]).astype(BF16)


def order_kernel(own_row, oth_row, log_ref, own_col, oth_col):
    core = lax.axis_index("c")
    for half, (row, col) in enumerate(((own_row, own_col), (oth_row, oth_col))):
        columns_of(row, col)
        for place in range(4):
            for slot in range(4):
                log_ref[place, slot, half] = col[rows_at(core, place, slot), :]


def local_log(log_ref, place):
    return log_ref[place].reshape(256, 128)[:, :1]


def mixture_kernel(places, own_ref, oth_ref, c_ref, log_ref, *outs):
    width = c_ref.shape[1]
    for place, out in zip(places, outs):
        for half, ref in enumerate((own_ref, oth_ref)):
            part = jnp.dot(
                ref[place].reshape(128, -1), c_ref[...], preferred_element_type=F32
            )
            out[:, half, :, :width] = part.reshape(4, 32, width).astype(out.dtype)
        if out.shape[-1] > width:
            log = pieces(local_log(log_ref, place), 3)
            out[:, :, :, width:] = log.reshape(4, 2, 32, EXT)


def first_merge_kernel(width, raw_ref, log_ref, r3_ref, r3_log, out_ref):
    value, log = merged(
        [raw_ref[...].reshape(256, width), r3_ref[...][..., :width].reshape(256, width).astype(F32)],
        [local_log(log_ref, 1), lse_of(r3_log)],
    )
    out_ref[:, :, :, :width] = value.astype(BF16).reshape(4, 2, 32, width)
    if out_ref.shape[-1] > width:
        out_ref[:, :, :, width:] = pieces(log, 3).reshape(4, 2, 32, EXT)


def second_merge_kernel(width, raw_ref, log_ref, r2_ref, r1_ref, r2_log, r1_log, *outs):
    for slot, out in enumerate(outs):
        value, log = merged(
            [raw_ref[slot].reshape(64, width)]
            + [r[slot][..., :width].reshape(64, width).astype(F32) for r in (r2_ref, r1_ref)],
            [log_ref[0, slot].reshape(64, 128)[:, :1]]
            + [
                jnp.sum(r[slot][..., -EXT:].reshape(64, EXT).astype(F32), axis=1, keepdims=True)
                for r in (r2_log, r1_log)
            ],
        )
        out[:, :, :width] = value.astype(BF16).reshape(2, 32, width)
        if out.shape[-1] > width:
            out[:, :, width:] = pieces(log, 3).reshape(2, 32, EXT)


def z_merge_kernel(width, *refs):
    got, logs, out = refs[:4], refs[4:8], refs[8]
    value, log = merged(
        [g[...][..., :width].reshape(64, width).astype(F32) for g in got],
        [lse_of(g) for g in logs],
    )
    out[:, :, :width] = value.reshape(2, 32, width)
    if out.shape[-1] > width:
        out[:, :, width:] = jnp.broadcast_to(log, (64, EXT)).reshape(2, 32, EXT)


def residual_kernel(stream, mine_ref, came_ref, mine_log, came_log, own_ref, oth_ref, out_ref):
    off, block = STREAMS[stream]
    width = 4 * block
    for half, rows in enumerate((own_ref, oth_ref)):
        value, log = merged(
            [mine_ref[half][:, :width], came_ref[1 - half][:, :width]],
            [mine_log[half][:, -EXT:][:, :1], came_log[1 - half][:, -EXT:][:, :1]],
        )
        for x in range(4):
            e = rows[:, 384 * x + off : 384 * x + off + block].astype(F32)
            cols = slice(block * x, block * x + block)
            out_ref[half, :, cols] = (e - value[:, cols]).astype(BF16)
        if out_ref.shape[-1] > width:
            out_ref[half, :, width:] = pieces(log, 3)


def turn_kernel(own_ref, oth_ref, rt_ref):
    for place in range(4):
        for half, ref in enumerate((own_ref, oth_ref)):
            at = place * 256 + half * 128
            rt_ref[:, at : at + 128] = ref[place].reshape(128, 1024).T


def gathered(width, places, refs, logs, log_ref, g_ref):
    for n, (place, ref, log) in enumerate(zip(places, refs, logs)):
        for half in range(2):
            at = n * 256 + half * 128
            whole = jnp.sum(
                log[:, half][..., -EXT:].reshape(128, EXT).astype(F32), axis=1, keepdims=True
            )
            share = jnp.exp(log_ref[place][:, half].reshape(128, 128)[:, :1] - whole)
            rows = ref[:, half][..., :width].reshape(128, width).astype(F32) * share
            g_ref[at : at + 128, :width] = rows.astype(BF16)
            if g_ref.shape[1] > width:
                g_ref[at : at + 128, width:] = pieces(share, 2)


def update_first_kernel(width, rt_ref, log_ref, g0_ref, g1_ref, l0, l1, u_ref, g_ref):
    gathered(width, (0, 1), (g0_ref, g1_ref), (l0, l1), log_ref, g_ref)
    for r in range(4):
        at = r * 256
        u_ref[at : at + 256, :] = jnp.dot(
            rt_ref[at : at + 256, :512], g_ref[...], preferred_element_type=F32
        )


def update_last_kernel(width, rt_ref, log_ref, g2_ref, g3_ref, l2, l3, u_ref, c_ref, *refs):
    gathered(width, (2, 3), (g2_ref, g3_ref), (l2, l3), log_ref, refs[-1])
    g_ref = refs[-1]
    if g_ref.shape[1] > width:
        keep_ref, send_ref, cnt_ref = refs[:3]
    else:
        cnt_ref, keep_ref, send_ref = refs[:3]
    core = lax.axis_index("c")
    for out, half in ((send_ref, 1 - core), (keep_ref, core)):
        for r in range(2):
            rows = pl.ds(pl.multiple_of(half * 512 + r * 256, 256), 256)
            u = u_ref[rows, :] + jnp.dot(
                rt_ref[rows, 512:], g_ref[...], preferred_element_type=F32
            )
            if g_ref.shape[1] > width:
                count = u[:, width : width + 1] + u[:, width + 1 : width + 2]
                cnt_ref[rows, :] = jnp.broadcast_to(count, (256, 128))
            count = cnt_ref[rows, :][:, :1]
            u = u[:, :width] + count * c_ref[rows, :].astype(F32)
            out[r * 256 : r * 256 + 256, :] = u.astype(out.dtype)


def split_kernel(keep_ref, recv_ref, p0_ref, p1_ref, p2_ref, p3_ref):
    core, x = lax.axis_index("c"), lax.axis_index("x")
    block = keep_ref.shape[1] // 4
    first = jnp.where(core == 0, 1, 3)
    second = jnp.where(core == 0, 3, 1)
    for out, mask in ((p3_ref, 2), (p2_ref, first), (p1_ref, second), (p0_ref, 0)):
        cols = pl.ds(pl.multiple_of(lax.bitwise_xor(x, mask) * block, 128), block)
        out[...] = (keep_ref[:, cols] + recv_ref[:, cols].astype(F32)).astype(out.dtype)


def moved_kernel(c_ref, p0_ref, a_ref, b_ref, moved_ref, square_ref):
    core, x = lax.axis_index("c"), lax.axis_index("x")
    block = p0_ref.shape[1]
    rows = pl.ds(pl.multiple_of(core * 512, 512), 512)
    cols = pl.ds(pl.multiple_of(x * block, 128), block)
    moved = c_ref[rows, cols].astype(F32) + p0_ref[...]
    moved = moved + a_ref[...].astype(F32) + b_ref[...].astype(F32)
    moved_ref[...] = moved
    square_ref[...] = to_row(jnp.sum(moved * moved, axis=1, keepdims=True))


def final_kernel(streams, *refs):
    moved, stats = refs[:streams], refs[streams : streams + 4]
    keep_ref, send_ref = refs[streams + 4 :]
    stat = stats[0][...] + stats[1][...] + stats[2][...] + stats[3][...]
    grown = 1.0 + stat[1:2]
    scale = to_column(lax.rsqrt(stat[:1] + 1e-06 * grown * grown))
    new = jnp.concatenate([m[...] * scale for m in moved], axis=1)
    low, high = new[:, :192], new[:, 192:]
    core = lax.axis_index("c")
    keep_ref[...] = jnp.where(core == 0, low, high)
    send_ref[...] = jnp.where(core == 0, high, low)


def per_device(embeddings, sharpness, centroids):
    d = embeddings.shape[1]
    part = functools.partial
    s, local, own_rows, *cols = scores(embeddings, centroids, sharpness)
    wide = ((1024, 128), F32)
    keep, send = call(weights_kernel, [((4, 4, 32, 1024), BF16)] * 2, s, local, scratch=[wide])
    other = swap_cores(send)
    (log,) = call(
        order_kernel, [((4, 4, 2, 32, 128), F32)], local, swap_cores(local), scratch=[wide] * 2
    )
    count = len(STREAMS)
    exts = [w + EXT if n == 0 else w for n, w in enumerate(WIDTHS)]

    r3, r2, r1, raw = [], [], [], []
    for n in range(count):
        m3, m2 = call(
            part(mixture_kernel, (3, 2)), [((4, 2, 32, exts[n]), BF16)] * 2, keep, other, cols[n], log
        )
        r3.append(cube(m3, "y", FIRST))
        r2.append(cube(m2, "y", FIRST))
        raw.append(
            call(
                part(mixture_kernel, (1, 0)), [((4, 2, 32, WIDTHS[n]), F32)] * 2,
                keep, other, cols[n], log,
            )
        )
    for n in range(count):
        (m1,) = call(
            part(first_merge_kernel, WIDTHS[n]), [((4, 2, 32, exts[n]), BF16)],
            raw[n][0], log, r3[n], r3[0],
        )
        r1.append(cube(m1, "y", SECOND))
    (rt,) = call(turn_kernel, [((1024, 1024), BF16)], keep, other)
    oth_rows = swap_cores(own_rows)
    got = []
    for n in range(count):
        summed = call(
            part(second_merge_kernel, WIDTHS[n]), [((2, 32, exts[n]), BF16)] * 4,
            raw[n][1], log, r2[n], r1[n], r2[0], r1[0],
        )
        got.append([shifted(summed[t], slot_shift(t)) for t in range(4)])

    both, came, pairs, g0, g1, g2, g3 = [], [], [], [], [], [], []
    for n in range(count):
        (one,) = call(
            part(z_merge_kernel, WIDTHS[n]), [((2, 32, exts[n]), F32)], *got[n], *got[0]
        )
        both.append(one)
        came.append(swap_cores(one))
        (pair,) = call(
            part(residual_kernel, n), [((2, 32, exts[n]), BF16)],
            both[n], came[n], both[0], came[0], own_rows, oth_rows,
        )
        pairs.append(pair)
        g0.append(
            jnp.stack([shifted(pair, tuple(-b for b in slot_shift(t))) for t in range(4)])
        )
    for n in range(count):
        g1.append(cube(g0[n], "y", SECOND))
        g2.append(cube(g0[n], "y", FIRST))
        g3.append(cube(g1[n], "y", FIRST))

    moved, squares = [], []
    for n in range(count):
        first = n == 0
        (u,) = call(
            part(update_first_kernel, WIDTHS[n]), [((1024, exts[n]), F32)],
            rt, log, g0[n], g1[n], g0[0], g1[0], scratch=[((512, exts[n]), BF16)],
        )
        outs = [((512, WIDTHS[n]), F32), ((512, WIDTHS[n]), BF16)]
        args = [rt, log, g2[n], g3[n], g2[0], g3[0], u, cols[n]]
        if first:
            keep_u, send_u, cnt = call(
                part(update_last_kernel, WIDTHS[n]), outs + [wide], *args,
                scratch=[((512, exts[n]), BF16)],
            )
        else:
            keep_u, send_u = call(
                part(update_last_kernel, WIDTHS[n]), outs, *args, cnt,
                scratch=[((512, exts[n]), BF16)],
            )
        block = WIDTHS[n] // 4
        p0, p1, p2, p3 = call(
            split_kernel,
            [((512, block), F32)] * 2 + [((512, block), BF16)] * 2,
            keep_u, swap_cores(send_u),
        )
        q3 = cube(p3, "x", FIRST)
        q2 = cube(p2, "x", FIRST)
        q1 = cube((p1 + q3.astype(F32)).astype(BF16), "x", SECOND)
        one, square = call(
            moved_kernel, [((512, block), F32), ((1, 512), F32)], cols[n], p0, q2, q1
        )
        moved.append(one)
        squares.append(square)
    cnt_row = cnt[:, 0].reshape(1, 1024)
    cnt_row = cnt_row + swap_cores(cnt_row)
    cnt_row = lax.dynamic_slice_in_dim(cnt_row, lax.axis_index("c") * 512, 512, 1)
    stat = jnp.concatenate([sum(squares), cnt_row])
    others = [
        lax.ppermute(stat, "x", [(i, (i + n) % 4) for i in range(4)]) for n in (1, 2, 3)
    ]
    kept, sent = call(part(final_kernel, count), [((512, 192), F32)] * 2, *moved, stat, *others)
    arrived = swap_cores(sent)
    low = lax.axis_index("c") == 0
    new = jnp.concatenate([jnp.where(low, kept, arrived), jnp.where(low, arrived, kept)])
    residual = jnp.concatenate(
        [
            pair[0, :, :w].reshape(32, 4, w // 4)
            for pair, w in zip(pairs, WIDTHS)
        ],
        axis=2,
    ).reshape(32, d)
    return (new, residual)


def solution(mesh):
    split = Mesh(mesh.devices.reshape(4, 2, 4, 8), ("x", "c", "y", "z"))
    rows, cents = ("x", "c"), ("y", "z")
    return jax.shard_map(
        per_device,
        mesh=split,
        in_specs=(P(rows, None), P(rows), P(cents, None)),
        out_specs=(P(cents, rows), P(rows + cents, None)),
        check_vma=False,
    )
```

```python
import functools

import jax
import jax.numpy as jnp
from jax import lax
from jax.experimental import pallas as pl
from jax.experimental.pallas import tpu as pltpu
from jax.sharding import Mesh
from jax.sharding import PartitionSpec as P


BF16, F32 = jnp.bfloat16, jnp.float32
VMEM = pl.BlockSpec(memory_space=pltpu.VMEM)
HBM = pl.BlockSpec(memory_space=pltpu.HBM)
PARAMS = pltpu.CompilerParams(vmem_limit_bytes=20 << 20)

EXT = 128
STREAMS = ((0, 256), (256, 128))
WIDTHS = tuple(4 * w for _, w in STREAMS)
EXTS = tuple(w + EXT if n == 0 else w for n, w in enumerate(WIDTHS))

FIRST, SECOND = (1, 3), (3, 1)
PAIR, NEAR, FAR = 1, 2, 6
QUEUE = (0, FAR, NEAR, NEAR ^ FAR, PAIR, PAIR ^ FAR, PAIR ^ NEAR, PAIR ^ NEAR ^ FAR)


def near(a):
    return pltpu.with_memory_space_constraint(a, pltpu.VMEM)


def call(kernel, outs, *args, scratch=(), far=0):
    hbm = [pltpu.with_memory_space_constraint(a, pltpu.HBM) for a in args[:far]]
    return pl.pallas_call(
        kernel,
        out_shape=[pltpu.VMEM(s, d) for s, d in outs],
        in_specs=[HBM] * far + [VMEM] * (len(args) - far),
        out_specs=[VMEM] * len(outs),
        scratch_shapes=[s if hasattr(s, "dtype") else pltpu.VMEM(*s) for s in scratch],
        compiler_params=PARAMS,
    )(*hbm, *(near(a) for a in args[far:]))


def to_column(row):
    return jnp.broadcast_to(row, (128, row.shape[1])).T[:, :1]


def to_row(column):
    return jnp.broadcast_to(column, (column.shape[0], 128)).T[:1, :]


def swap_cores(a):
    return lax.ppermute(a, "c", [(0, 1), (1, 0)])


def cube(a, axis, masks):
    pairs = [(c, i, i ^ masks[c]) for c in range(2) for i in range(4)]
    if axis == "x":
        return lax.ppermute(a, ("x", "c"), [(i * 2 + c, j * 2 + c) for c, i, j in pairs])
    return lax.ppermute(a, ("c", axis), [(c * 4 + i, c * 4 + j) for c, i, j in pairs])


def along_z(a, mask):
    pairs = [(c * 8 + z, c * 8 + (((z - c) % 8) ^ mask) % 8) for c in range(2) for z in range(8)]
    pairs = [(s, s // 8 * 8 + (t % 8 + s // 8) % 8) for s, t in pairs]
    return lax.ppermute(a, ("c", "z"), pairs)


def lse_of(ref):
    ext = ref[...][..., -EXT:].reshape(-1, EXT).astype(F32)
    return jnp.sum(ext, axis=1, keepdims=True)


def kept_log(ref):
    return ref[...][..., -EXT:].reshape(-1, EXT)[:, :1]


def pieces(value, count):
    lane = lax.broadcasted_iota(jnp.int32, (value.shape[0], EXT), 1)
    out = jnp.zeros(lane.shape, F32)
    for n in range(count):
        part = value.astype(BF16).astype(F32)
        out = jnp.where(lane == n, part, out)
        value = value - part
    return out.astype(BF16)


def merged(values, logs):
    top = functools.reduce(jnp.maximum, logs)
    parts = [jnp.exp(one - top) for one in logs]
    total = sum(parts)
    inverse = 1.0 / total
    value = sum(v * (p * inverse) for v, p in zip(values, parts))
    return value, top + jnp.log(total)


def masks_of_core():
    core = lax.axis_index("c")
    return jnp.where(core == 0, FIRST[0], FIRST[1]), jnp.where(core == 0, SECOND[0], SECOND[1])


def natural_row(block):
    core, y, z = lax.axis_index("c"), lax.axis_index("y"), lax.axis_index("z")
    place, n = block // 8, lax.rem(block, 8)
    first, second = masks_of_core()
    mask = jnp.where(place == 1, second, jnp.where(place == 2, first, jnp.where(place == 3, 2, 0)))
    step = 0
    for k, m in enumerate(QUEUE):
        step = jnp.where(n == k, m, step)
    label = lax.bitwise_xor(lax.rem(z - core + 8, 8), step)
    return pl.multiple_of((lax.bitwise_xor(y, mask) * 8 + lax.rem(label + core, 8)) * 32, 32)


def local_softmax(place, e_ref, c_ref, sharp_ref, p_ref, log_ref, at):
    rows = slice(place * 256, place * 256 + 256)
    s = lax.dot_general(
        e_ref[rows, :], c_ref[...], (((1,), (1,)), ((), ())), preferred_element_type=F32
    )
    s = s * sharp_ref[rows, :][:, :1]
    top = jnp.max(s, axis=1, keepdims=True)
    weights = jnp.exp(s - top)
    total = jnp.sum(weights, axis=1, keepdims=True)
    p_ref[at] = (weights * (1.0 / total)).astype(BF16)
    log_ref[at] = jnp.broadcast_to(top + jnp.log(total), (256, 128))


def mixture(p_ref, at, c_ref, out):
    def chunk(j, carry):
        cols = pl.ds(pl.multiple_of(j * 256, 256), 256)
        part = jnp.dot(p_ref[at], c_ref[:, cols], preferred_element_type=F32)
        out[:, :, cols] = part.reshape(8, 32, 256).astype(out.dtype)
        return carry

    lax.fori_loop(0, c_ref.shape[1] // 256, chunk, 0)


def front_kernel(e_hbm, c_hbm, sharp_row, *refs):
    e_ref, c_ref, sharp_ref, p_ref, log_ref = refs[:5]
    col_refs = refs[5 : 5 + len(STREAMS)]
    m3_ref, m2_ref = refs[5 + len(STREAMS) : 7 + len(STREAMS)]
    sharp_col, e_sems, c_sem, col_sems = refs[-4:]

    def block_copy(block):
        return pltpu.make_async_copy(
            e_hbm.at[pl.ds(natural_row(block), 32)],
            e_ref.at[pl.ds(pl.multiple_of(block * 32, 32), 32)],
            e_sems.at[block],
        )

    def start(n, carry):
        block_copy(31 - n).start()
        return carry

    def wait(n, carry):
        block_copy(n).wait()
        return carry

    lax.fori_loop(0, 8, start, 0)
    whole = pltpu.make_async_copy(c_hbm, c_ref, c_sem)
    whole.start()
    lax.fori_loop(8, 32, start, 0)
    copies = []
    for n, (ref, (off, width)) in enumerate(zip(col_refs, STREAMS)):
        for x in range(4):
            copies.append(
                pltpu.make_async_copy(
                    c_hbm.at[:, pl.ds(384 * x + off, width)],
                    ref.at[:, pl.ds(width * x, width)],
                    col_sems.at[n * 4 + x],
                )
            )
    for copy in copies:
        copy.start()
    for r in range(0, 1024, 256):
        sharp_col[r : r + 256, :] = jnp.broadcast_to(sharp_row[:, r : r + 256], (128, 256)).T

    def order(block, carry):
        at = pl.ds(pl.multiple_of(block * 32, 32), 32)
        sharp_ref[at, :] = sharp_col[pl.ds(natural_row(block), 32), :]
        return carry

    lax.fori_loop(0, 32, order, 0)
    lax.fori_loop(24, 32, wait, 0)
    whole.wait()
    local_softmax(3, e_ref, c_ref, sharp_ref, p_ref, log_ref, 1)
    lax.fori_loop(16, 24, wait, 0)
    local_softmax(2, e_ref, c_ref, sharp_ref, p_ref, log_ref, 0)
    for copy in copies:
        copy.wait()
    for at, out in ((1, m3_ref), (0, m2_ref)):
        mixture(p_ref, at, col_refs[0], out)
        out[:, :, WIDTHS[0] :] = pieces(log_ref[at][:, :1], 3).reshape(8, 32, EXT)
    lax.fori_loop(0, 16, wait, 0)


def back_kernel(e_ref, c_ref, sharp_ref, col_ref, p_ref, log_ref, raw1_ref, raw0_ref):
    for place in (1, 0):
        local_softmax(place, e_ref, c_ref, sharp_ref, p_ref, log_ref, place)
    mixture(p_ref, 1, col_ref, raw1_ref)
    mixture(p_ref, 0, col_ref, raw0_ref)


def mixture_kernel(p_ref, c_ref, high_ref, low_ref):
    mixture(p_ref, 1, c_ref, high_ref)
    mixture(p_ref, 0, c_ref, low_ref)


def values_of(ref, width):
    return ref[...][..., :width].reshape(-1, width).astype(F32)


def put(ref, width, value, log):
    shape = ref.shape[:-1]
    ref[..., :width] = value.astype(ref.dtype).reshape(*shape, width)
    if ref.shape[-1] > width:
        ext = pieces(log, 3) if ref.dtype == BF16 else jnp.broadcast_to(log, (log.shape[0], EXT))
        ref[..., width:] = ext.reshape(*shape, EXT)


def first_merge_kernel(width, raw_ref, log_ref, r3_ref, r3_log, out_ref):
    value, log = merged(
        [values_of(raw_ref, width), values_of(r3_ref, width)],
        [log_ref[1][:, :1], lse_of(r3_log)],
    )
    put(out_ref, width, value, log)


def second_merge_kernel(width, raw_ref, log_ref, r2_ref, r1_ref, r2_log, r1_log, send_ref, keep_ref):
    for half, out in enumerate((keep_ref, send_ref)):
        blocks = pl.ds(4 * half, 4)
        value, log = merged(
            [values_of(r.at[blocks], width) for r in (raw_ref, r2_ref, r1_ref)],
            [log_ref[0][128 * half : 128 * half + 128, :1]]
            + [lse_of(r.at[blocks]) for r in (r2_log, r1_log)],
        )
        put(out, width, value, log)


def z_merge_kernel(width, mine_ref, came_ref, mine_log, came_log, send_ref, keep_ref):
    came = lse_of(came_log) if came_log.dtype == BF16 else kept_log(came_log)
    value, log = merged(
        [values_of(mine_ref, width), values_of(came_ref, width)], [kept_log(mine_log), came]
    )
    half = value.shape[0] // 2
    put(keep_ref, width, value[:half], log[:half])
    put(send_ref, width, value[half:], log[half:])


def residual_kernel(stream, mine_ref, came_ref, mine_log, came_log, e_ref, out_ref):
    off, block = STREAMS[stream]
    width = 4 * block
    value, log = merged(
        [values_of(mine_ref, width), values_of(came_ref, width)],
        [kept_log(mine_log), kept_log(came_log)],
    )
    rows = [e_ref[:32, 384 * x + off : 384 * x + off + block].astype(F32) for x in range(4)]
    put(out_ref, width, jnp.concatenate(rows, axis=1) - value, log)


def turn_kernel(low_ref, high_ref, rt_ref):
    for n, ref in enumerate((low_ref, high_ref)):
        for at in range(2):
            rt_ref[:, n * 512 + at * 256 : n * 512 + at * 256 + 256] = ref[at].T


def gathered(width, refs, logs, log_ref, g_ref):
    for n, (ref, log) in enumerate(zip(refs, logs)):
        at = slice(n * 256, n * 256 + 256)
        share = jnp.exp(log_ref[n][:, :1] - lse_of(log))
        g_ref[at, :width] = (values_of(ref, width) * share).astype(BF16)
        if g_ref.shape[1] > width:
            g_ref[at, width:] = pieces(share, 2)


def update_first_kernel(width, rt_ref, log_ref, g0_ref, g1_ref, l0, l1, u_ref, g_ref):
    gathered(width, (g0_ref, g1_ref), (l0, l1), log_ref, g_ref)

    def chunk(r, carry):
        rows = pl.ds(pl.multiple_of(r * 256, 256), 256)
        u_ref[rows, :] = jnp.dot(rt_ref[rows, :512], g_ref[...], preferred_element_type=F32)
        return carry

    lax.fori_loop(0, 4, chunk, 0)


def update_half(width, half, rt_ref, g_ref, u_ref, c_ref, cnt_ref, own_count, out):
    def chunk(r, carry):
        to = pl.ds(pl.multiple_of(r * 256, 256), 256)
        rows = pl.ds(pl.multiple_of(half * 512 + r * 256, 256), 256)
        u = u_ref[rows, :] + jnp.dot(rt_ref[rows, 512:], g_ref[...], preferred_element_type=F32)
        if own_count:
            count = u[:, width : width + 1] + u[:, width + 1 : width + 2]
            cnt_ref[to, :] = jnp.broadcast_to(count, (256, 128))
        count = cnt_ref[to, :][:, :1]
        out[to, :width] = (u[:, :width] + count * c_ref[rows, :].astype(F32)).astype(out.dtype)
        if out.shape[1] > width:
            out[to, width:] = pieces(count, 3)
        return carry

    lax.fori_loop(0, 2, chunk, 0)


def update_send_kernel(width, own_count, rt_ref, log_ref, g2_ref, g3_ref, l2, l3, u_ref, c_ref, *refs):
    cnt_ref, send_ref, g_ref = refs if not own_count else (refs[2], refs[0], refs[1])
    gathered(width, (g2_ref, g3_ref), (l2, l3), log_ref, g_ref)
    half = 1 - lax.axis_index("c")
    update_half(width, half, rt_ref, g_ref, u_ref, c_ref, cnt_ref, own_count, send_ref)


def update_keep_kernel(width, own_count, rt_ref, g_ref, u_ref, c_ref, *refs):
    cnt_ref, keep_ref = refs if not own_count else refs[::-1]
    half = lax.axis_index("c")
    update_half(width, half, rt_ref, g_ref, u_ref, c_ref, cnt_ref, own_count, keep_ref)


def split_kernel(width, keep_ref, recv_ref, cnt_ref, p0_ref, p1_ref, p2_ref, p3_ref, *count_row):
    x = lax.axis_index("x")
    block = width // 4
    first, second = masks_of_core()
    for out, mask in ((p3_ref, 2), (p2_ref, first), (p1_ref, second), (p0_ref, 0)):
        cols = pl.ds(pl.multiple_of(lax.bitwise_xor(x, mask) * block, 128), block)
        out[...] = (keep_ref[:, cols] + recv_ref[:, cols].astype(F32)).astype(out.dtype)
    for out in count_row:
        out[...] = to_row(cnt_ref[...][:, :1] + lse_of(recv_ref))


def moved_kernel(c_ref, p0_ref, a_ref, b_ref, *refs):
    moved_ref, square_ref = refs[-2:]
    core, x = lax.axis_index("c"), lax.axis_index("x")
    block = p0_ref.shape[1]
    rows = pl.ds(pl.multiple_of(core * 512, 512), 512)
    cols = pl.ds(pl.multiple_of(x * block, 128), block)
    moved = c_ref[rows, cols].astype(F32) + p0_ref[...]
    moved = moved + a_ref[...].astype(F32) + b_ref[...].astype(F32)
    moved_ref[...] = moved
    square = to_row(jnp.sum(moved * moved, axis=1, keepdims=True))
    if len(refs) > 2:
        square = jnp.concatenate([square + refs[0][...], refs[1][...]], axis=0)
    square_ref[...] = square


def final_kernel(streams, *refs):
    moved, stats = refs[:streams], refs[streams : streams + 4]
    keep_ref, send_ref = refs[streams + 4 :]
    stat = stats[0][...] + stats[1][...] + stats[2][...] + stats[3][...]
    grown = 1.0 + stat[1:2]
    scale = to_column(lax.rsqrt(stat[:1] + 1e-06 * grown * grown))
    new = jnp.concatenate([m[...] * scale for m in moved], axis=1)
    low, high = new[:, :192], new[:, 192:]
    core = lax.axis_index("c")
    keep_ref[...] = jnp.where(core == 0, low, high)
    send_ref[...] = jnp.where(core == 0, high, low)


def per_device(embeddings, sharpness, centroids):
    rows, d = embeddings.shape
    k = centroids.shape[0]
    part = functools.partial
    every = range(len(STREAMS))
    wide = ((rows, 128), F32)
    half_p, half_log = ((2, 256, k), BF16), ((2, 256, 128), F32)

    def message(blocks, n, dtype=BF16, bare=False):
        return ((blocks, 32, WIDTHS[n] if bare else EXTS[n]), dtype)

    e, c, sharp, p_high, log_high, *rest = call(
        front_kernel,
        [((rows, d), BF16), ((k, d), BF16), wide, half_p, half_log]
        + [((k, w), BF16) for w in WIDTHS] + [message(8, 0)] * 2,
        embeddings, centroids, sharpness.reshape(1, rows), far=2,
        scratch=[
            wide, pltpu.SemaphoreType.DMA((32,)), pltpu.SemaphoreType.DMA,
            pltpu.SemaphoreType.DMA((4 * len(STREAMS),)),
        ],
    )
    cols, sent = rest[: len(STREAMS)], [rest[len(STREAMS) :]]
    p_low, log_low, *raw0 = call(
        back_kernel, [half_p, half_log] + [message(8, 0, F32, True)] * 2,
        e, c, sharp, cols[0],
    )
    raw = [raw0]
    for n in every[1:]:
        sent.append(call(mixture_kernel, [message(8, n)] * 2, p_high, cols[n]))
        raw.append(call(mixture_kernel, [message(8, n, F32, True)] * 2, p_low, cols[n]))

    r3 = [cube(sent[n][0], "y", FIRST) for n in every]
    r2 = [cube(sent[n][1], "y", FIRST) for n in every]
    r1 = []
    for n in every:
        (m1,) = call(
            part(first_merge_kernel, WIDTHS[n]), [message(8, n)],
            raw[n][0], log_low, r3[n], r3[0],
        )
        r1.append(cube(m1, "y", SECOND))
    (rt,) = call(turn_kernel, [((k, rows), BF16)], p_low, p_high)
    mine, came = [], []
    for n in every:
        send, keep = call(
            part(second_merge_kernel, WIDTHS[n]), [message(4, n), message(4, n, F32)],
            raw[n][1], log_low, r2[n], r1[n], r2[0], r1[0],
        )
        mine.append([keep])
        came.append([along_z(send, PAIR)])
    for step, mask in ((1, NEAR), (2, FAR)):
        blocks = 4 >> step
        for n in every:
            send, keep = call(
                part(z_merge_kernel, WIDTHS[n]),
                [message(blocks, n, BF16 if step == 1 else F32), message(blocks, n, F32)],
                mine[n][-1], came[n][-1], mine[0][step - 1], came[0][step - 1],
            )
            mine[n].append(keep)
            came[n].append(along_z(send, mask))

    own, g0, g1, g2, g3 = [], [], [], [], []
    for n in every:
        (g,) = call(
            part(residual_kernel, n), [message(1, n)],
            mine[n][-1], came[n][-1], mine[0][-1], came[0][-1], e,
        )
        own.append(g)
        for mask in (FAR, NEAR, PAIR):
            g = jnp.concatenate([g, along_z(g, mask)])
        g0.append(g)
        g1.append(cube(g, "y", SECOND))
        g2.append(cube(g, "y", FIRST))
        g3.append(cube(g1[n], "y", FIRST))

    moved, square, counts = [], [], []
    for n in every:
        width, first = WIDTHS[n], n == 0
        g_shape = ((512, EXTS[n]), BF16)
        (u,) = call(
            part(update_first_kernel, width), [((k, EXTS[n]), F32)],
            rt, log_low, g0[n], g1[n], g0[0], g1[0], scratch=[g_shape],
        )
        tall = [((512, 128), F32)] if first else []
        send, g, *cnt = call(
            part(update_send_kernel, width, first),
            [((512, EXTS[n]), BF16), g_shape] + tall,
            rt, log_high, g2[n], g3[n], g2[0], g3[0], u, cols[n], *counts[:1],
        )
        counts += cnt
        keep, *cnt = call(
            part(update_keep_kernel, width, first),
            [((512, width), F32)] + tall, rt, g, u, cols[n], *counts[1:],
        )
        counts += cnt
        block = width // 4
        p0, p1, p2, p3, *row = call(
            part(split_kernel, width),
            [((512, block), F32)] * 2 + [((512, block), BF16)] * 2
            + ([((1, 512), F32)] if first else []),
            keep, swap_cores(send), counts[1],
        )
        if first:
            count_row = row
        q3 = cube(p3, "x", FIRST)
        q2 = cube(p2, "x", FIRST)
        q1 = cube((p1 + q3.astype(F32)).astype(BF16), "x", SECOND)
        last = n == len(STREAMS) - 1
        one, some = call(
            moved_kernel, [((512, block), F32), ((2 if last else 1, 512), F32)],
            cols[n], p0, q2, q1, *(square + count_row if last else []),
        )
        moved.append(one)
        square = [some]
    stat = square[0]
    others = [lax.ppermute(stat, "x", [(i, (i + n) % 4) for i in range(4)]) for n in (1, 2, 3)]
    kept, sent = call(
        part(final_kernel, len(STREAMS)), [((512, 192), F32)] * 2, *moved, stat, *others
    )
    arrived = swap_cores(sent)
    low = lax.axis_index("c") == 0
    new = jnp.concatenate([jnp.where(low, kept, arrived), jnp.where(low, arrived, kept)])
    residual = jnp.concatenate(
        [g[0, :, :w].reshape(32, 4, w // 4) for g, w in zip(own, WIDTHS)], axis=2
    ).reshape(32, d)
    return (new, residual)


def solution(mesh):
    split = Mesh(mesh.devices.reshape(4, 2, 4, 8), ("x", "c", "y", "z"))
    rows, cents = ("x", "c"), ("y", "z")
    return jax.shard_map(
        per_device,
        mesh=split,
        in_specs=(P(rows, None), P(rows), P(cents, None)),
        out_specs=(P(cents, rows), P(rows + cents, None)),
        check_vma=False,
    )
```

```python
import functools

import jax
import jax.numpy as jnp
from jax import lax
from jax.experimental import pallas as pl
from jax.experimental.pallas import tpu as pltpu
from jax.sharding import Mesh
from jax.sharding import PartitionSpec as P


BF16, F32 = jnp.bfloat16, jnp.float32
VMEM = pl.BlockSpec(memory_space=pltpu.VMEM)
HBM = pl.BlockSpec(memory_space=pltpu.HBM)
PARAMS = pltpu.CompilerParams(vmem_limit_bytes=20 << 20)

EXT = 128
STREAMS = ((0, 256), (256, 128))
WIDTHS = tuple(4 * w for _, w in STREAMS)
EXTS = tuple(w + EXT if n == 0 else w for n, w in enumerate(WIDTHS))
LAST = len(STREAMS) - 1
GATHER_EXTS = tuple(w + EXT if n == LAST else w for n, w in enumerate(WIDTHS))

FIRST, SECOND = (1, 3), (3, 1)
PAIR, NEAR, FAR = 1, 2, 6


def near(a):
    return pltpu.with_memory_space_constraint(a, pltpu.VMEM)


def call(kernel, outs, *args, scratch=(), far=0):
    hbm = [pltpu.with_memory_space_constraint(a, pltpu.HBM) for a in args[:far]]
    return pl.pallas_call(
        kernel,
        out_shape=[pltpu.VMEM(s, d) for s, d in outs],
        in_specs=[HBM] * far + [VMEM] * (len(args) - far),
        out_specs=[VMEM] * len(outs),
        scratch_shapes=[s if hasattr(s, "dtype") else pltpu.VMEM(*s) for s in scratch],
        compiler_params=PARAMS,
    )(*hbm, *(near(a) for a in args[far:]))


def to_column(row):
    return jnp.broadcast_to(row, (128, row.shape[1])).T[:, :1]


def to_row(column):
    return jnp.broadcast_to(column, (column.shape[0], 128)).T[:1, :]


def swap_cores(a):
    return lax.ppermute(a, "c", [(0, 1), (1, 0)])


def cube(a, axis, masks):
    pairs = [(c, i, i ^ masks[c]) for c in range(2) for i in range(4)]
    if axis == "x":
        return lax.ppermute(a, ("x", "c"), [(i * 2 + c, j * 2 + c) for c, i, j in pairs])
    return lax.ppermute(a, ("c", axis), [(c * 4 + i, c * 4 + j) for c, i, j in pairs])


def along_z(a, mask):
    pairs = [(c * 8 + z, c * 8 + (((z - c) % 8) ^ mask) % 8) for c in range(2) for z in range(8)]
    pairs = [(s, s // 8 * 8 + (t % 8 + s // 8) % 8) for s, t in pairs]
    return lax.ppermute(a, ("c", "z"), pairs)


def lse_of(ref):
    ext = ref[...][..., -EXT:].reshape(-1, EXT).astype(F32)
    return jnp.sum(ext, axis=1, keepdims=True)


def kept_log(ref):
    return ref[...][..., -EXT:].reshape(-1, EXT)[:, :1]


def pieces(value, count):
    lane = lax.broadcasted_iota(jnp.int32, (value.shape[0], EXT), 1)
    out = jnp.zeros(lane.shape, F32)
    for n in range(count):
        part = value.astype(BF16).astype(F32)
        out = jnp.where(lane == n, part, out)
        value = value - part
    return out.astype(BF16)


def merged(values, logs):
    top = functools.reduce(jnp.maximum, logs)
    parts = [jnp.exp(one - top) for one in logs]
    total = sum(parts)
    inverse = 1.0 / total
    value = sum(v * (p * inverse) for v, p in zip(values, parts))
    return value, top + jnp.log(total)


def masks_of_core():
    core = lax.axis_index("c")
    return jnp.where(core == 0, FIRST[0], FIRST[1]), jnp.where(core == 0, SECOND[0], SECOND[1])


def natural_row(block):
    core, y, z = lax.axis_index("c"), lax.axis_index("y"), lax.axis_index("z")
    place, n = block // 8, lax.rem(block, 8)
    first, second = masks_of_core()
    mask = lax.bitwise_xor(lax.rem(place, 2) * second, place // 2 * first)
    low = lax.bitwise_xor(lax.rem(n, 2) * FAR, lax.rem(n // 2, 2) * NEAR)
    step = lax.bitwise_xor(low, n // 4 * PAIR)
    label = lax.bitwise_xor(lax.rem(z - core + 8, 8), step)
    return pl.multiple_of((lax.bitwise_xor(y, mask) * 8 + lax.rem(label + core, 8)) * 32, 32)


def local_softmax(place, e_ref, c_ref, sharp_ref, p_ref, log_ref, at):
    rows = slice(place * 256, place * 256 + 256)
    s = lax.dot_general(
        e_ref[rows, :], c_ref[...], (((1,), (1,)), ((), ())), preferred_element_type=F32
    )
    s = s * sharp_ref[rows, :][:, :1]
    top = jnp.max(s, axis=1, keepdims=True)
    weights = jnp.exp(s - top)
    total = jnp.sum(weights, axis=1, keepdims=True)
    p_ref[at] = (weights * (1.0 / total)).astype(BF16)
    log_ref[at] = jnp.broadcast_to(top + jnp.log(total), (256, 128))


def mixture(p_ref, at, c_ref, out):
    def chunk(j, carry):
        cols = pl.ds(pl.multiple_of(j * 256, 256), 256)
        part = jnp.dot(p_ref[at], c_ref[:, cols], preferred_element_type=F32)
        out[:, :, cols] = part.reshape(8, 32, 256).astype(out.dtype)
        return carry

    lax.fori_loop(0, c_ref.shape[1] // 256, chunk, 0)


def front_kernel(e_hbm, c_hbm, sharp_hbm, *refs):
    e_ref, c_ref, sharp_ref, p_ref, log_ref = refs[:5]
    col_refs = refs[5 : 5 + len(STREAMS)]
    m3_ref, m2_ref = refs[5 + len(STREAMS) : 7 + len(STREAMS)]
    sharp_row, sharp_col, e_sems, c_sem, sharp_sem, col_sems = refs[-6:]

    def block_copy(block):
        return pltpu.make_async_copy(
            e_hbm.at[pl.ds(natural_row(block), 32)],
            e_ref.at[pl.ds(pl.multiple_of(block * 32, 32), 32)],
            e_sems.at[block],
        )

    def start(n, carry):
        block_copy(31 - n).start()
        return carry

    def wait(n, carry):
        block_copy(n).wait()
        return carry

    sharps = pltpu.make_async_copy(sharp_hbm, sharp_row, sharp_sem)
    sharps.start()
    lax.fori_loop(0, 8, start, 0)
    whole = pltpu.make_async_copy(c_hbm, c_ref, c_sem)
    whole.start()
    lax.fori_loop(8, 32, start, 0)
    copies = []
    for n, (ref, (off, width)) in enumerate(zip(col_refs, STREAMS)):
        for x in range(4):
            copies.append(
                pltpu.make_async_copy(
                    c_hbm.at[:, pl.ds(384 * x + off, width)],
                    ref.at[:, pl.ds(width * x, width)],
                    col_sems.at[n * 4 + x],
                )
            )
    for copy in copies:
        copy.start()
    sharps.wait()
    for r in range(0, 1024, 256):
        sharp_col[r : r + 256, :] = jnp.broadcast_to(sharp_row[:, r : r + 256], (128, 256)).T

    def order(block, carry):
        at = pl.ds(pl.multiple_of(block * 32, 32), 32)
        sharp_ref[at, :] = sharp_col[pl.ds(natural_row(block), 32), :]
        return carry

    lax.fori_loop(0, 32, order, 0)
    lax.fori_loop(24, 32, wait, 0)
    whole.wait()
    local_softmax(3, e_ref, c_ref, sharp_ref, p_ref, log_ref, 1)
    lax.fori_loop(16, 24, wait, 0)
    local_softmax(2, e_ref, c_ref, sharp_ref, p_ref, log_ref, 0)
    for copy in copies:
        copy.wait()
    for at, out in ((1, m3_ref), (0, m2_ref)):
        mixture(p_ref, at, col_refs[0], out)
        out[:, :, WIDTHS[0] :] = pieces(log_ref[at][:, :1], 3).reshape(8, 32, EXT)
    lax.fori_loop(0, 16, wait, 0)


def back_kernel(e_ref, c_ref, sharp_ref, col_ref, p_ref, log_ref, raw1_ref, raw0_ref):
    for place in (1, 0):
        local_softmax(place, e_ref, c_ref, sharp_ref, p_ref, log_ref, place)
    mixture(p_ref, 1, col_ref, raw1_ref)
    mixture(p_ref, 0, col_ref, raw0_ref)


def mixture_kernel(p_ref, c_ref, high_ref, low_ref):
    mixture(p_ref, 1, c_ref, high_ref)
    mixture(p_ref, 0, c_ref, low_ref)


def values_of(ref, width):
    return ref[...][..., :width].reshape(-1, width).astype(F32)


def put(ref, width, value, log):
    shape = ref.shape[:-1]
    ref[..., :width] = value.astype(ref.dtype).reshape(*shape, width)
    if ref.shape[-1] > width:
        ext = pieces(log, 3) if ref.dtype == BF16 else jnp.broadcast_to(log, (log.shape[0], EXT))
        ref[..., width:] = ext.reshape(*shape, EXT)


def first_merge_kernel(width, raw_ref, log_ref, r3_ref, r3_log, out_ref):
    value, log = merged(
        [values_of(raw_ref, width), values_of(r3_ref, width)],
        [log_ref[1][:, :1], lse_of(r3_log)],
    )
    put(out_ref, width, value, log)


def second_merge_kernel(width, raw_ref, log_ref, r2_ref, r1_ref, r2_log, r1_log, send_ref, keep_ref):
    for half, out in enumerate((keep_ref, send_ref)):
        blocks = pl.ds(4 * half, 4)
        value, log = merged(
            [values_of(r.at[blocks], width) for r in (raw_ref, r2_ref, r1_ref)],
            [log_ref[0][128 * half : 128 * half + 128, :1]]
            + [lse_of(r.at[blocks]) for r in (r2_log, r1_log)],
        )
        put(out, width, value, log)


def z_merge_kernel(width, mine_ref, came_ref, mine_log, came_log, send_ref, keep_ref):
    came = lse_of(came_log) if came_log.dtype == BF16 else kept_log(came_log)
    value, log = merged(
        [values_of(mine_ref, width), values_of(came_ref, width)], [kept_log(mine_log), came]
    )
    half = value.shape[0] // 2
    put(keep_ref, width, value[:half], log[:half])
    put(send_ref, width, value[half:], log[half:])


def residual_kernel(stream, mine_ref, came_ref, mine_log, came_log, e_ref, out_ref):
    off, block = STREAMS[stream]
    width = 4 * block
    value, log = merged(
        [values_of(mine_ref, width), values_of(came_ref, width)],
        [kept_log(mine_log), kept_log(came_log)],
    )
    rows = [e_ref[:32, 384 * x + off : 384 * x + off + block].astype(F32) for x in range(4)]
    put(out_ref, width, jnp.concatenate(rows, axis=1) - value, log)


def turn_kernel(low_ref, high_ref, rt_ref):
    for n, ref in enumerate((low_ref, high_ref)):
        for at in range(2):
            rt_ref[:, n * 512 + at * 256 : n * 512 + at * 256 + 256] = ref[at].T


def gathered(width, refs, logs, log_ref, g_ref):
    for n, (ref, log) in enumerate(zip(refs, logs)):
        at = slice(n * 256, n * 256 + 256)
        share = jnp.exp(log_ref[n][:, :1] - lse_of(log))
        g_ref[at, :width] = (values_of(ref, width) * share).astype(BF16)
        if g_ref.shape[1] > width:
            g_ref[at, width:] = pieces(share, 2)


def update_first_kernel(width, rt_ref, log_ref, g0_ref, g1_ref, l0, l1, u_ref, g_ref):
    gathered(width, (g0_ref, g1_ref), (l0, l1), log_ref, g_ref)

    def chunk(r, carry):
        rows = pl.ds(pl.multiple_of(r * 256, 256), 256)
        u_ref[rows, :] = jnp.dot(rt_ref[rows, :512], g_ref[...], preferred_element_type=F32)
        return carry

    lax.fori_loop(0, 4, chunk, 0)


def update_half(width, half, rt_ref, g_ref, u_ref, c_ref, cnt_ref, own_count, out):
    def chunk(r, carry):
        to = pl.ds(pl.multiple_of(r * 256, 256), 256)
        rows = pl.ds(pl.multiple_of(half * 512 + r * 256, 256), 256)
        u = u_ref[rows, :] + jnp.dot(rt_ref[rows, 512:], g_ref[...], preferred_element_type=F32)
        if own_count:
            count = u[:, width : width + 1] + u[:, width + 1 : width + 2]
            cnt_ref[to, :] = jnp.broadcast_to(count, (256, 128))
        count = cnt_ref[to, :][:, :1]
        out[to, :width] = (u[:, :width] + count * c_ref[rows, :].astype(F32)).astype(out.dtype)
        if out.shape[1] > width:
            out[to, width:] = pieces(count, 3)
        return carry

    lax.fori_loop(0, 2, chunk, 0)


def update_send_kernel(width, own_count, rt_ref, log_ref, g2_ref, g3_ref, l2, l3, u_ref, c_ref, *refs):
    cnt_ref, send_ref, g_ref = refs if not own_count else (refs[2], refs[0], refs[1])
    gathered(width, (g2_ref, g3_ref), (l2, l3), log_ref, g_ref)
    half = 1 - lax.axis_index("c")
    update_half(width, half, rt_ref, g_ref, u_ref, c_ref, cnt_ref, own_count, send_ref)


def update_keep_kernel(width, own_count, rt_ref, g_ref, u_ref, c_ref, *refs):
    cnt_ref, keep_ref = refs if not own_count else refs[::-1]
    half = lax.axis_index("c")
    update_half(width, half, rt_ref, g_ref, u_ref, c_ref, cnt_ref, own_count, keep_ref)


def split_kernel(width, keep_ref, recv_ref, cnt_ref, p0_ref, p1_ref, p2_ref, p3_ref, *count_row):
    x = lax.axis_index("x")
    block = width // 4
    first, second = masks_of_core()
    for out, mask in ((p3_ref, 2), (p2_ref, first), (p1_ref, second), (p0_ref, 0)):
        cols = pl.ds(pl.multiple_of(lax.bitwise_xor(x, mask) * block, 128), block)
        out[...] = (keep_ref[:, cols] + recv_ref[:, cols].astype(F32)).astype(out.dtype)
    for out in count_row:
        out[...] = to_row(cnt_ref[...][:, :1] + lse_of(recv_ref))


def moved_kernel(c_ref, p0_ref, a_ref, b_ref, *refs):
    moved_ref, square_ref = refs[-2:]
    core, x = lax.axis_index("c"), lax.axis_index("x")
    block = p0_ref.shape[1]
    rows = pl.ds(pl.multiple_of(core * 512, 512), 512)
    cols = pl.ds(pl.multiple_of(x * block, 128), block)
    moved = c_ref[rows, cols].astype(F32) + p0_ref[...]
    moved = moved + a_ref[...].astype(F32) + b_ref[...].astype(F32)
    moved_ref[...] = moved
    square = to_row(jnp.sum(moved * moved, axis=1, keepdims=True))
    if len(refs) > 2:
        square = jnp.concatenate([square + refs[0][...], refs[1][...]], axis=0)
    square_ref[...] = square


def final_kernel(streams, *refs):
    moved, stats = refs[:streams], refs[streams : streams + 4]
    keep_ref, send_ref = refs[streams + 4 :]
    stat = stats[0][...] + stats[1][...] + stats[2][...] + stats[3][...]
    grown = 1.0 + stat[1:2]
    scale = to_column(lax.rsqrt(stat[:1] + 1e-06 * grown * grown))
    new = jnp.concatenate([(m[...] * scale).T for m in moved], axis=0)
    low, high = new[:192], new[192:]
    core = lax.axis_index("c")
    keep_ref[...] = jnp.where(core == 0, low, high)
    send_ref[...] = jnp.where(core == 0, high, low)


def per_device(embeddings, sharpness, centroids):
    rows, d = embeddings.shape
    k = centroids.shape[0]
    part = functools.partial
    every = range(len(STREAMS))
    wide = ((rows, 128), F32)
    half_p, half_log = ((2, 256, k), BF16), ((2, 256, 128), F32)

    def message(blocks, n, dtype=BF16, bare=False):
        return ((blocks, 32, WIDTHS[n] if bare else EXTS[n]), dtype)

    e, c, sharp, p_high, log_high, *rest = call(
        front_kernel,
        [((rows, d), BF16), ((k, d), BF16), wide, half_p, half_log]
        + [((k, w), BF16) for w in WIDTHS] + [message(8, 0)] * 2,
        embeddings, centroids, sharpness.reshape(1, rows), far=3,
        scratch=[
            ((1, rows), F32), wide, pltpu.SemaphoreType.DMA((32,)),
            pltpu.SemaphoreType.DMA, pltpu.SemaphoreType.DMA,
            pltpu.SemaphoreType.DMA((4 * len(STREAMS),)),
        ],
    )
    cols, sent = rest[: len(STREAMS)], [rest[len(STREAMS) :]]
    p_low, log_low, *raw0 = call(
        back_kernel, [half_p, half_log] + [message(8, 0, F32, True)] * 2,
        e, c, sharp, cols[0],
    )
    raw = [raw0]
    for n in every[1:]:
        sent.append(call(mixture_kernel, [message(8, n)] * 2, p_high, cols[n]))
        raw.append(call(mixture_kernel, [message(8, n, F32, True)] * 2, p_low, cols[n]))

    r3 = [cube(sent[n][0], "y", FIRST) for n in every]
    r2 = [cube(sent[n][1], "y", FIRST) for n in every]
    r1 = []
    for n in every:
        (m1,) = call(
            part(first_merge_kernel, WIDTHS[n]), [message(8, n)],
            raw[n][0], log_low, r3[n], r3[0],
        )
        r1.append(cube(m1, "y", SECOND))
    (rt,) = call(turn_kernel, [((k, rows), BF16)], p_low, p_high)
    mine, came = [], []
    for n in every:
        send, keep = call(
            part(second_merge_kernel, WIDTHS[n]), [message(4, n), message(4, n, F32)],
            raw[n][1], log_low, r2[n], r1[n], r2[0], r1[0],
        )
        mine.append([keep])
        came.append([along_z(send, PAIR)])
    for step, mask in ((1, NEAR), (2, FAR)):
        blocks = 4 >> step
        for n in every:
            send, keep = call(
                part(z_merge_kernel, WIDTHS[n]),
                [message(blocks, n, BF16 if step == 1 else F32), message(blocks, n, F32)],
                mine[n][-1], came[n][-1], mine[0][step - 1], came[0][step - 1],
            )
            mine[n].append(keep)
            came[n].append(along_z(send, mask))

    own, g0, g1, g2, g3 = [], [], [], [], []
    for n in every:
        (g,) = call(
            part(residual_kernel, n), [((1, 32, GATHER_EXTS[n]), BF16)],
            mine[n][-1], came[n][-1], mine[0][-1], came[0][-1], e,
        )
        own.append(g)
        for mask in (FAR, NEAR, PAIR):
            g = jnp.concatenate([g, along_z(g, mask)])
        g0.append(g)
        g1.append(cube(g, "y", SECOND))
        g2.append(cube(g, "y", FIRST))
        g3.append(cube(g1[n], "y", FIRST))

    moved, square, counts = [], [], []
    for n in reversed(every):
        width, first = WIDTHS[n], n == LAST
        g_shape = ((512, GATHER_EXTS[n]), BF16)
        (u,) = call(
            part(update_first_kernel, width), [((k, GATHER_EXTS[n]), F32)],
            rt, log_low, g0[n], g1[n], g0[LAST], g1[LAST], scratch=[g_shape],
        )
        tall = [((512, 128), F32)] if first else []
        send, g, *cnt = call(
            part(update_send_kernel, width, first),
            [((512, GATHER_EXTS[n]), BF16), g_shape] + tall,
            rt, log_high, g2[n], g3[n], g2[LAST], g3[LAST], u, cols[n], *counts[:1],
        )
        counts += cnt
        keep, *cnt = call(
            part(update_keep_kernel, width, first),
            [((512, width), F32)] + tall, rt, g, u, cols[n], *counts[1:],
        )
        counts += cnt
        block = width // 4
        p0, p1, p2, p3, *row = call(
            part(split_kernel, width),
            [((512, block), F32)] * 2 + [((512, block), BF16)] * 2
            + ([((1, 512), F32)] if first else []),
            keep, swap_cores(send), counts[1],
        )
        if first:
            count_row = row
        q3 = cube(p3, "x", FIRST)
        q2 = cube(p2, "x", FIRST)
        q1 = cube((p1 + q3.astype(F32)).astype(BF16), "x", SECOND)
        last = n == 0
        one, some = call(
            moved_kernel, [((512, block), F32), ((2 if last else 1, 512), F32)],
            cols[n], p0, q2, q1, *(square + count_row if last else []),
        )
        moved.insert(0, one)
        square = [some]
    stat = square[0]
    others = [lax.ppermute(stat, "x", [(i, (i + n) % 4) for i in range(4)]) for n in (1, 2, 3)]
    kept, sent = call(
        part(final_kernel, len(STREAMS)), [((192, 512), F32)] * 2, *moved, stat, *others
    )
    arrived = swap_cores(sent)
    low = lax.axis_index("c") == 0
    halves = [jnp.where(low, kept, arrived), jnp.where(low, arrived, kept)]
    new = jnp.concatenate(halves, axis=1).T
    residual = jnp.concatenate(
        [g[0, :, :w].reshape(32, 4, w // 4) for g, w in zip(own, WIDTHS)], axis=2
    ).reshape(32, d)
    return (new, residual)


def solution(mesh):
    split = Mesh(mesh.devices.reshape(4, 2, 4, 8), ("x", "c", "y", "z"))
    rows, cents = ("x", "c"), ("y", "z")
    return jax.shard_map(
        per_device,
        mesh=split,
        in_specs=(P(rows, None), P(rows), P(cents, None)),
        out_specs=(P(cents, rows), P(rows + cents, None)),
        check_vma=False,
    )
```

```python
import functools

import jax
import jax.numpy as jnp
from jax import lax
from jax.experimental import pallas as pl
from jax.experimental.pallas import tpu as pltpu
from jax.sharding import Mesh
from jax.sharding import PartitionSpec as P


BF16, F32 = jnp.bfloat16, jnp.float32
VMEM = pl.BlockSpec(memory_space=pltpu.VMEM)
HBM = pl.BlockSpec(memory_space=pltpu.HBM)
PARAMS = pltpu.CompilerParams(vmem_limit_bytes=20 << 20)

EXT = 128
STREAMS = ((0, 256), (256, 128))
WIDTHS = tuple(4 * w for _, w in STREAMS)
EXTS = tuple(w + EXT if n == 0 else w for n, w in enumerate(WIDTHS))

FIRST, SECOND = (1, 3), (3, 1)
PAIR, NEAR, FAR = 1, 2, 6


def near(a):
    return pltpu.with_memory_space_constraint(a, pltpu.VMEM)


def call(kernel, outs, *args, scratch=(), far=0):
    hbm = [pltpu.with_memory_space_constraint(a, pltpu.HBM) for a in args[:far]]
    return pl.pallas_call(
        kernel,
        out_shape=[pltpu.VMEM(s, d) for s, d in outs],
        in_specs=[HBM] * far + [VMEM] * (len(args) - far),
        out_specs=[VMEM] * len(outs),
        scratch_shapes=[s if hasattr(s, "dtype") else pltpu.VMEM(*s) for s in scratch],
        compiler_params=PARAMS,
    )(*hbm, *(near(a) for a in args[far:]))


def to_column(row):
    return jnp.broadcast_to(row, (128, row.shape[1])).T[:, :1]


def to_row(column):
    return jnp.broadcast_to(column, (column.shape[0], 128)).T[:1, :]


def swap_cores(a):
    return lax.ppermute(a, "c", [(0, 1), (1, 0)])


def cube(a, axis, masks):
    pairs = [(c, i, i ^ masks[c]) for c in range(2) for i in range(4)]
    if axis == "x":
        return lax.ppermute(a, ("x", "c"), [(i * 2 + c, j * 2 + c) for c, i, j in pairs])
    return lax.ppermute(a, ("c", axis), [(c * 4 + i, c * 4 + j) for c, i, j in pairs])


def along_z(a, mask):
    pairs = [(c * 8 + z, c * 8 + (((z - c) % 8) ^ mask) % 8) for c in range(2) for z in range(8)]
    pairs = [(s, s // 8 * 8 + (t % 8 + s // 8) % 8) for s, t in pairs]
    return lax.ppermute(a, ("c", "z"), pairs)


def lse_of(ref):
    ext = ref[...][..., -EXT:].reshape(-1, EXT).astype(F32)
    return jnp.sum(ext, axis=1, keepdims=True)


def kept_log(ref):
    return ref[...][..., -EXT:].reshape(-1, EXT)[:, :1]


def pieces(value, count):
    lane = lax.broadcasted_iota(jnp.int32, (value.shape[0], EXT), 1)
    out = jnp.zeros(lane.shape, F32)
    for n in range(count):
        part = value.astype(BF16).astype(F32)
        out = jnp.where(lane == n, part, out)
        value = value - part
    return out.astype(BF16)


def merged(values, logs):
    top = functools.reduce(jnp.maximum, logs)
    parts = [jnp.exp(one - top) for one in logs]
    total = sum(parts)
    inverse = 1.0 / total
    value = sum(v * (p * inverse) for v, p in zip(values, parts))
    return value, top + jnp.log(total)


def masks_of_core():
    core = lax.axis_index("c")
    return jnp.where(core == 0, FIRST[0], FIRST[1]), jnp.where(core == 0, SECOND[0], SECOND[1])


def natural_row(block):
    core, y, z = lax.axis_index("c"), lax.axis_index("y"), lax.axis_index("z")
    place, n = block // 8, lax.rem(block, 8)
    first, second = masks_of_core()
    mask = lax.bitwise_xor(lax.rem(place, 2) * second, place // 2 * first)
    low = lax.bitwise_xor(lax.rem(n, 2) * FAR, lax.rem(n // 2, 2) * NEAR)
    step = lax.bitwise_xor(low, n // 4 * PAIR)
    label = lax.bitwise_xor(lax.rem(z - core + 8, 8), step)
    return pl.multiple_of((lax.bitwise_xor(y, mask) * 8 + lax.rem(label + core, 8)) * 32, 32)


def local_softmax(place, e_ref, c_ref, sharp_ref, p_ref, log_ref, at):
    rows = slice(place * 256, place * 256 + 256)
    s = lax.dot_general(
        e_ref[rows, :], c_ref[...], (((1,), (1,)), ((), ())), preferred_element_type=F32
    )
    s = s * sharp_ref[rows, :][:, :1]
    top = jnp.max(s, axis=1, keepdims=True)
    weights = jnp.exp(s - top)
    total = jnp.sum(weights, axis=1, keepdims=True)
    p_ref[at] = (weights * (1.0 / total)).astype(BF16)
    log_ref[at] = jnp.broadcast_to(top + jnp.log(total), (256, 128))


def mixture(p_ref, at, c_ref, out, step=256):
    def chunk(j, carry):
        cols = pl.ds(pl.multiple_of(j * 256, 256), 256)
        some = pl.ds(pl.multiple_of(j * step, 128), 256)
        part = jnp.dot(p_ref[at], c_ref[:, some], preferred_element_type=F32)
        out[:, :, cols] = part.reshape(8, 32, 256).astype(out.dtype)
        return carry

    lax.fori_loop(0, c_ref.shape[1] // step, chunk, 0)


def first_message(place, e_ref, c_ref, sharp_ref, p_ref, log_ref, m_ref):
    local_softmax(place, e_ref, c_ref, sharp_ref, p_ref, log_ref, 0)
    mixture(p_ref, 0, c_ref, m_ref, 384)
    m_ref[:, :, WIDTHS[0] :] = pieces(log_ref[0][:, :1], 3).reshape(8, 32, EXT)


def front_kernel(e_hbm, c_hbm, sharp_hbm, e_ref, c_ref, sharp_ref, p_ref, log_ref, m_ref, *refs):
    sharp_row, sharp_col, e_sems, c_sem, sharp_sem = refs

    def block_copy(block):
        return pltpu.make_async_copy(
            e_hbm.at[pl.ds(natural_row(block), 32)],
            e_ref.at[pl.ds(pl.multiple_of(block * 32, 32), 32)],
            e_sems.at[block],
        )

    def start(n, carry):
        block_copy(31 - n).start()
        return carry

    def wait(n, carry):
        block_copy(n).wait()
        return carry

    whole = pltpu.make_async_copy(c_hbm, c_ref, c_sem)
    sharps = pltpu.make_async_copy(sharp_hbm, sharp_row, sharp_sem)
    whole.start()
    sharps.start()
    lax.fori_loop(0, 32, start, 0)
    sharps.wait()
    for r in range(0, 1024, 256):
        sharp_col[r : r + 256, :] = jnp.broadcast_to(sharp_row[:, r : r + 256], (128, 256)).T

    def order(block, carry):
        at = pl.ds(pl.multiple_of(block * 32, 32), 32)
        sharp_ref[at, :] = sharp_col[pl.ds(natural_row(block), 32), :]
        return carry

    lax.fori_loop(0, 32, order, 0)
    lax.fori_loop(24, 32, wait, 0)
    whole.wait()
    first_message(3, e_ref, c_ref, sharp_ref, p_ref, log_ref, m_ref)
    lax.fori_loop(0, 24, wait, 0)


def middle_kernel(c_hbm, e_ref, c_ref, sharp_ref, p_ref, log_ref, m_ref, *refs):
    col_refs, sems = refs[:-1], refs[-1]
    copies = []
    for n, (ref, (off, width)) in enumerate(zip(col_refs, STREAMS)):
        for x in range(4):
            copies.append(
                pltpu.make_async_copy(
                    c_hbm.at[:, pl.ds(384 * x + off, width)],
                    ref.at[:, pl.ds(width * x, width)],
                    sems.at[n * 4 + x],
                )
            )
    for copy in copies:
        copy.start()
    first_message(2, e_ref, c_ref, sharp_ref, p_ref, log_ref, m_ref)
    for copy in copies:
        copy.wait()


def back_kernel(place, e_ref, c_ref, sharp_ref, p_ref, log_ref, raw_ref):
    local_softmax(place, e_ref, c_ref, sharp_ref, p_ref, log_ref, 0)
    mixture(p_ref, 0, c_ref, raw_ref, 384)


def mixture_kernel(high_p, low_p, c_ref, high_ref, low_ref):
    mixture(high_p, 0, c_ref, high_ref)
    mixture(low_p, 0, c_ref, low_ref)


def values_of(ref, width):
    return ref[...][..., :width].reshape(-1, width).astype(F32)


def put(ref, width, value, log):
    shape = ref.shape[:-1]
    ref[..., :width] = value.astype(ref.dtype).reshape(*shape, width)
    if ref.shape[-1] > width:
        ext = pieces(log, 3) if ref.dtype == BF16 else jnp.broadcast_to(log, (log.shape[0], EXT))
        ref[..., width:] = ext.reshape(*shape, EXT)


def first_merge_kernel(width, raw_ref, log_ref, r3_ref, r3_log, out_ref):
    value, log = merged(
        [values_of(raw_ref, width), values_of(r3_ref, width)],
        [log_ref[0][:, :1], lse_of(r3_log)],
    )
    put(out_ref, width, value, log)


def second_merge_kernel(width, raw_ref, log_ref, r2_ref, r1_ref, r2_log, r1_log, send_ref, keep_ref):
    for half, out in enumerate((keep_ref, send_ref)):
        blocks = pl.ds(4 * half, 4)
        value, log = merged(
            [values_of(r.at[blocks], width) for r in (raw_ref, r2_ref, r1_ref)],
            [log_ref[0][128 * half : 128 * half + 128, :1]]
            + [lse_of(r.at[blocks]) for r in (r2_log, r1_log)],
        )
        put(out, width, value, log)


def z_merge_kernel(width, mine_ref, came_ref, mine_log, came_log, send_ref, keep_ref):
    came = lse_of(came_log) if came_log.dtype == BF16 else kept_log(came_log)
    value, log = merged(
        [values_of(mine_ref, width), values_of(came_ref, width)], [kept_log(mine_log), came]
    )
    half = value.shape[0] // 2
    put(keep_ref, width, value[:half], log[:half])
    put(send_ref, width, value[half:], log[half:])


def residual_kernel(stream, mine_ref, came_ref, mine_log, came_log, e_ref, out_ref):
    off, block = STREAMS[stream]
    width = 4 * block
    value, log = merged(
        [values_of(mine_ref, width), values_of(came_ref, width)],
        [kept_log(mine_log), kept_log(came_log)],
    )
    rows = [e_ref[:32, 384 * x + off : 384 * x + off + block].astype(F32) for x in range(4)]
    put(out_ref, width, jnp.concatenate(rows, axis=1) - value, log)


def turn_kernel(*refs):
    rt_ref = refs[-1]
    for n, ref in enumerate(refs[:-1]):
        rt_ref[:, n * 256 : n * 256 + 256] = ref[0].T


def gathered(width, refs, logs, local_logs, g_ref):
    for n, (ref, log, local) in enumerate(zip(refs, logs, local_logs)):
        at = slice(n * 256, n * 256 + 256)
        share = jnp.exp(local[0][:, :1] - lse_of(log))
        g_ref[at, :width] = (values_of(ref, width) * share).astype(BF16)
        if g_ref.shape[1] > width:
            g_ref[at, width:] = pieces(share, 2)


def update_first_kernel(width, rt_ref, log0, log1, g0_ref, g1_ref, l0, l1, u_ref, g_ref):
    gathered(width, (g0_ref, g1_ref), (l0, l1), (log0, log1), g_ref)

    def chunk(r, carry):
        rows = pl.ds(pl.multiple_of(r * 256, 256), 256)
        u_ref[rows, :] = jnp.dot(rt_ref[rows, :512], g_ref[...], preferred_element_type=F32)
        return carry

    lax.fori_loop(0, 4, chunk, 0)


def update_half(width, half, rt_ref, g_ref, u_ref, c_ref, cnt_ref, own_count, out):
    def chunk(r, carry):
        to = pl.ds(pl.multiple_of(r * 256, 256), 256)
        rows = pl.ds(pl.multiple_of(half * 512 + r * 256, 256), 256)
        u = u_ref[rows, :] + jnp.dot(rt_ref[rows, 512:], g_ref[...], preferred_element_type=F32)
        if own_count:
            count = u[:, width : width + 1] + u[:, width + 1 : width + 2]
            cnt_ref[to, :] = jnp.broadcast_to(count, (256, 128))
        count = cnt_ref[to, :][:, :1]
        out[to, :width] = (u[:, :width] + count * c_ref[rows, :].astype(F32)).astype(out.dtype)
        if out.shape[1] > width:
            out[to, width:] = pieces(count, 3)
        return carry

    lax.fori_loop(0, 2, chunk, 0)


def update_send_kernel(
    width, own_count, rt_ref, log2, log3, g2_ref, g3_ref, l2, l3, u_ref, c_ref, *refs
):
    cnt_ref, send_ref, g_ref = refs if not own_count else (refs[2], refs[0], refs[1])
    gathered(width, (g2_ref, g3_ref), (l2, l3), (log2, log3), g_ref)
    half = 1 - lax.axis_index("c")
    update_half(width, half, rt_ref, g_ref, u_ref, c_ref, cnt_ref, own_count, send_ref)


def update_keep_kernel(width, own_count, rt_ref, g_ref, u_ref, c_ref, *refs):
    cnt_ref, keep_ref = refs if not own_count else refs[::-1]
    half = lax.axis_index("c")
    update_half(width, half, rt_ref, g_ref, u_ref, c_ref, cnt_ref, own_count, keep_ref)


def split_kernel(width, keep_ref, recv_ref, cnt_ref, p0_ref, p1_ref, p2_ref, p3_ref, *count_row):
    x = lax.axis_index("x")
    block = width // 4
    first, second = masks_of_core()
    for out, mask in ((p3_ref, 2), (p2_ref, first), (p1_ref, second), (p0_ref, 0)):
        cols = pl.ds(pl.multiple_of(lax.bitwise_xor(x, mask) * block, 128), block)
        out[...] = (keep_ref[:, cols] + recv_ref[:, cols].astype(F32)).astype(out.dtype)
    for out in count_row:
        out[...] = to_row(cnt_ref[...][:, :1] + lse_of(recv_ref))


def moved_kernel(c_ref, p0_ref, a_ref, b_ref, *refs):
    moved_ref, square_ref = refs[-2:]
    core, x = lax.axis_index("c"), lax.axis_index("x")
    block = p0_ref.shape[1]
    rows = pl.ds(pl.multiple_of(core * 512, 512), 512)
    cols = pl.ds(pl.multiple_of(x * block, 128), block)
    moved = c_ref[rows, cols].astype(F32) + p0_ref[...]
    moved = moved + a_ref[...].astype(F32) + b_ref[...].astype(F32)
    moved_ref[...] = moved
    square = to_row(jnp.sum(moved * moved, axis=1, keepdims=True))
    if len(refs) > 2:
        square = jnp.concatenate([square + refs[0][...], refs[1][...]], axis=0)
    square_ref[...] = square


def final_kernel(streams, *refs):
    moved, stats = refs[:streams], refs[streams : streams + 4]
    keep_ref, send_ref = refs[streams + 4 :]
    stat = stats[0][...] + stats[1][...] + stats[2][...] + stats[3][...]
    grown = 1.0 + stat[1:2]
    scale = to_column(lax.rsqrt(stat[:1] + 1e-06 * grown * grown))
    new = jnp.concatenate([(m[...] * scale).T for m in moved], axis=0)
    low, high = new[:192], new[192:]
    core = lax.axis_index("c")
    keep_ref[...] = jnp.where(core == 0, low, high)
    send_ref[...] = jnp.where(core == 0, high, low)


def per_device(embeddings, sharpness, centroids):
    rows, d = embeddings.shape
    k = centroids.shape[0]
    part = functools.partial
    every = range(len(STREAMS))
    wide = ((rows, 128), F32)
    one_p, one_log = ((1, 256, k), BF16), ((1, 256, 128), F32)

    def message(blocks, n, dtype=BF16, bare=False):
        return ((blocks, 32, WIDTHS[n] if bare else EXTS[n]), dtype)

    e, c, sharp, p3, log3, m3 = call(
        front_kernel,
        [((rows, d), BF16), ((k, d), BF16), wide, one_p, one_log, message(8, 0)],
        embeddings, centroids, sharpness.reshape(1, rows), far=3,
        scratch=[
            ((1, rows), F32), wide, pltpu.SemaphoreType.DMA((32,)),
            pltpu.SemaphoreType.DMA, pltpu.SemaphoreType.DMA,
        ],
    )
    p2, log2, m2, *cols = call(
        middle_kernel,
        [one_p, one_log, message(8, 0)] + [((k, w), BF16) for w in WIDTHS],
        centroids, e, c, sharp, far=1,
        scratch=[pltpu.SemaphoreType.DMA((4 * len(STREAMS),))],
    )
    sent = [[m3, m2]]
    p1, log1, raw1 = call(
        part(back_kernel, 1), [one_p, one_log, message(8, 0, F32, True)], e, c, sharp
    )
    p0, log0, raw0 = call(
        part(back_kernel, 0), [one_p, one_log, message(8, 0, F32, True)], e, c, sharp
    )
    raw = [[raw1, raw0]]
    for n in every[1:]:
        sent.append(call(mixture_kernel, [message(8, n)] * 2, p3, p2, cols[n]))
        raw.append(call(mixture_kernel, [message(8, n, F32, True)] * 2, p1, p0, cols[n]))

    r3 = [cube(sent[n][0], "y", FIRST) for n in every]
    r2 = [cube(sent[n][1], "y", FIRST) for n in every]
    r1 = []
    for n in every:
        (m1,) = call(
            part(first_merge_kernel, WIDTHS[n]), [message(8, n)],
            raw[n][0], log1, r3[n], r3[0],
        )
        r1.append(cube(m1, "y", SECOND))
    (rt,) = call(turn_kernel, [((k, rows), BF16)], p0, p1, p2, p3)
    mine, came = [], []
    for n in every:
        send, keep = call(
            part(second_merge_kernel, WIDTHS[n]), [message(4, n), message(4, n, F32)],
            raw[n][1], log0, r2[n], r1[n], r2[0], r1[0],
        )
        mine.append([keep])
        came.append([along_z(send, PAIR)])
    for step, mask in ((1, NEAR), (2, FAR)):
        blocks = 4 >> step
        for n in every:
            send, keep = call(
                part(z_merge_kernel, WIDTHS[n]),
                [message(blocks, n, BF16 if step == 1 else F32), message(blocks, n, F32)],
                mine[n][-1], came[n][-1], mine[0][step - 1], came[0][step - 1],
            )
            mine[n].append(keep)
            came[n].append(along_z(send, mask))

    own, g0, g1, g2, g3 = [], [], [], [], []
    for n in every:
        (g,) = call(
            part(residual_kernel, n), [((1, 32, EXTS[n]), BF16)],
            mine[n][-1], came[n][-1], mine[0][-1], came[0][-1], e,
        )
        own.append(g)
        for mask in (FAR, NEAR, PAIR):
            g = jnp.concatenate([g, along_z(g, mask)])
        g0.append(g)
        g1.append(cube(g, "y", SECOND))
        g2.append(cube(g, "y", FIRST))
        g3.append(cube(g1[n], "y", FIRST))

    moved, square, counts = [], [], []
    for n in every:
        width, first = WIDTHS[n], n == 0
        g_shape = ((512, EXTS[n]), BF16)
        (u,) = call(
            part(update_first_kernel, width), [((k, EXTS[n]), F32)],
            rt, log0, log1, g0[n], g1[n], g0[0], g1[0], scratch=[g_shape],
        )
        tall = [((512, 128), F32)] if first else []
        send, g, *cnt = call(
            part(update_send_kernel, width, first),
            [((512, EXTS[n]), BF16), g_shape] + tall,
            rt, log2, log3, g2[n], g3[n], g2[0], g3[0], u, cols[n], *counts[:1],
        )
        counts += cnt
        keep, *cnt = call(
            part(update_keep_kernel, width, first),
            [((512, width), F32)] + tall, rt, g, u, cols[n], *counts[1:],
        )
        counts += cnt
        block = width // 4
        s0, s1, s2, s3, *row = call(
            part(split_kernel, width),
            [((512, block), F32)] * 2 + [((512, block), BF16)] * 2
            + ([((1, 512), F32)] if first else []),
            keep, swap_cores(send), counts[1],
        )
        if first:
            count_row = row
        q3 = cube(s3, "x", FIRST)
        q2 = cube(s2, "x", FIRST)
        q1 = cube((s1 + q3.astype(F32)).astype(BF16), "x", SECOND)
        last = n == len(STREAMS) - 1
        one, some = call(
            moved_kernel, [((512, block), F32), ((2 if last else 1, 512), F32)],
            cols[n], s0, q2, q1, *(square + count_row if last else []),
        )
        moved.append(one)
        square = [some]
    stat = square[0]
    others = [lax.ppermute(stat, "x", [(i, (i + n) % 4) for i in range(4)]) for n in (1, 2, 3)]
    kept, sent = call(
        part(final_kernel, len(STREAMS)), [((192, 512), F32)] * 2, *moved, stat, *others
    )
    arrived = swap_cores(sent)
    low = lax.axis_index("c") == 0
    halves = [jnp.where(low, kept, arrived), jnp.where(low, arrived, kept)]
    new = jnp.concatenate(halves, axis=1).T
    residual = jnp.concatenate(
        [g[0, :, :w].reshape(32, 4, w // 4) for g, w in zip(own, WIDTHS)], axis=2
    ).reshape(32, d)
    return (new, residual)


def solution(mesh):
    split = Mesh(mesh.devices.reshape(4, 2, 4, 8), ("x", "c", "y", "z"))
    rows, cents = ("x", "c"), ("y", "z")
    return jax.shard_map(
        per_device,
        mesh=split,
        in_specs=(P(rows, None), P(rows), P(cents, None)),
        out_specs=(P(cents, rows), P(rows + cents, None)),
        check_vma=False,
    )
```
